256 devices in a mesh: doc: 16 (over z, y_lo), leaf: 16 (over x, y_hi, core).
Axes of the slice: x: 4, y: 4 (y_hi: 2, y_lo: 2; y = y_hi * 2 + y_lo), z: 8, core: 2. Of those that a mesh axis runs over, the one named last changes fastest.
Arguments:
- features: bfloat16 [262144, 256], P(('doc', 'leaf'))
- scores: float32 [262144], P(('doc', 'leaf')), may hold values from -6 to 6
- labels: int32 [262144], P(('doc', 'leaf')), may hold values from 0 to 4
- query_ids: int32 [262144], P(('doc', 'leaf')), may hold values from 0 to 8186, as said below
- ranks: int32 [262144], P(('doc', 'leaf')), may hold values from 1 to 128, as said below
- leaf_ids: int32 [262144], P(('doc', 'leaf')), may hold values from 0 to 15
Outputs:
- gradients: float32 [262144], P(('doc', 'leaf'))
- tree_output: float32 [262144], P(('doc', 'leaf'))
- new_scores: float32 [262144], P(('doc', 'leaf'))
The draws below stay inside these ranges and needn't reach their ends.
Inputs may be any that keep to these rules, and one draw needn't show every extreme that they name: `query_ids`: the rows of one query are contiguous; ids are 0 on the first row and rise by one at each new query; a query has 1 to 128 rows and some query has exactly 128. Within each query the ranks of its rows are the numbers 1 to its row count, each once.
All inputs are finite; a program needn't handle non-finite values.
Results may differ from the reference program's by a relative error of at most 0.0038.
Values sent between devices are 32-bit elements; how exact they have to be, the bound alone decides.
A program may use at most 64 MiB of HBM per device.

```python
import math
import jax
import jax.numpy as jnp
import numpy as np
from jax import lax

F = 256
LEAVES = 16
MAXQ = 128
ROWS_DEV = 1024
ROWS = 262144


def shared_rows(key):
    key_parts = jax.random.split(jax.random.fold_in(key, 7001), 6)
    frame_total = ROWS // MAXQ + 1
    frame_phase = jax.random.randint(key_parts[0], (), 1, MAXQ)
    full_frame = (jax.random.randint(key_parts[1], (), 1, ROWS // ROWS_DEV) * ROWS_DEV + frame_phase) // MAXQ
    cut_scores = jax.random.randint(key_parts[2], (frame_total, MAXQ - 1), 0, 1024) * MAXQ + jnp.arange(MAXQ - 1)[None, :]
    cut_points = (jnp.argsort(cut_scores, axis=1)[:, :3] + 1).astype(jnp.int32)
    frame_numbers = jnp.arange(frame_total)
    cut_count = jnp.where((frame_numbers == full_frame) | (frame_numbers == 0) | (frame_numbers == frame_total - 1), 0, 3)
    positions = jnp.arange(ROWS)
    shifted = positions + frame_phase
    frame_index = shifted // MAXQ
    frame_offset = shifted % MAXQ
    chosen = (cut_points[frame_index] == frame_offset[:, None]) & (jnp.arange(3)[None, :] < cut_count[frame_index][:, None])
    new_query = (frame_offset == 0) | (positions == 0) | jnp.any(chosen, axis=1)
    query_ids = (jnp.cumsum(new_query.astype(jnp.int32)) - 1).astype(jnp.int32)
    order_key = (jax.random.randint(key_parts[4], (ROWS,), 0, MAXQ) * MAXQ + frame_offset).astype(jnp.int32)
    frame_query = lax.dynamic_update_slice(jnp.full((frame_total * MAXQ,), -1, jnp.int32), query_ids, (frame_phase,)).reshape(frame_total, MAXQ)
    frame_key = lax.dynamic_update_slice(jnp.zeros((frame_total * MAXQ,), jnp.int32), order_key, (frame_phase,)).reshape(frame_total, MAXQ)
    earlier = (frame_query[:, None, :] == frame_query[:, :, None]) & (frame_key[:, None, :] < frame_key[:, :, None])
    frame_rank = 1 + jnp.sum(earlier.astype(jnp.int32), axis=2)
    rank_values = lax.dynamic_slice(frame_rank.reshape(-1), (frame_phase,), (ROWS,)).astype(jnp.int32)
    grade_draw = jax.random.randint(key_parts[5], (ROWS,), 0, 16)
    label_values = (grade_draw >= 8).astype(jnp.int32) + (grade_draw >= 12).astype(jnp.int32) + (grade_draw >= 14).astype(jnp.int32) + (grade_draw >= 15).astype(jnp.int32)
    return (query_ids, rank_values, label_values)


def draw_query_ids(key, part):
    return shared_rows(key)[0]


def draw_ranks(key, part):
    return shared_rows(key)[1]


def draw_labels(key, part):
    return shared_rows(key)[2]


def draw_features(key, part):
    label_values = shared_rows(key)[2].astype(jnp.float32)
    key_parts = jax.random.split(jax.random.fold_in(key, 7002), 4)
    common = jax.random.normal(key_parts[1], (ROWS,), jnp.float32)
    shared_dir = jax.random.normal(key_parts[2], (F,), jnp.float32)
    label_dir = 0.5 * jax.random.normal(key_parts[3], (F,), jnp.float32)
    noise = jax.random.normal(key_parts[0], (ROWS, F), jnp.float32)
    common_scale = 0.5
    values = noise + common_scale * common[:, None] * shared_dir[None, :] + 0.5 * (label_values - 1.0)[:, None] * label_dir[None, :]
    return values.astype(jnp.bfloat16)


def with_ends(values, own_key, least, largest):
    index_at = [jax.random.randint(jax.random.fold_in(own_key, axis), (), 0, length) for axis, length in enumerate(values.shape)]
    widest = values.shape.index(max(values.shape))
    beside = index_at[:widest] + [(index_at[widest] + 1) % values.shape[widest]] + index_at[widest + 1:]
    return values.at[tuple(index_at)].set(least).at[tuple(beside)].set(largest)


def block_scale(stream_key, dims, cuts, low, top_value):
    def one(dim, shards_of):
        steps = jax.random.uniform(jax.random.fold_in(jax.random.fold_in(stream_key, 6), dim), (shards_of,), jnp.float32, low / len(cuts), top_value / len(cuts))
        return jnp.repeat(jnp.exp(steps), dims[dim] // shards_of).reshape((-1,) + (1,) * (len(dims) - dim - 1))

    factor_of = one(*cuts[0])
    for cut in cuts[1:]:
        factor_of = factor_of * one(*cut)
    return factor_of


def cumulative_ranks(count, skew):
    weights = [(1 << 20) // math.isqrt(grade ** skew) + 1 for grade in range(1, count + 1)]
    deviation = 1 + sum(weights) // (1 << 30)
    return np.cumsum(np.array([max(1, weight // deviation) for weight in weights]))


def ranked_ids(key, shape, count, slope):
    table = cumulative_ranks(count, slope)
    lot = jax.random.randint(jax.random.fold_in(key, 1), shape, 0, int(table[count - 1]))
    grade = jnp.searchsorted(jnp.asarray(table, jnp.int32), lot, side="right")
    return jax.random.permutation(jax.random.fold_in(key, 2), count)[grade].astype(jnp.int32)


def centred(stream_key, dims, spread, reach, shards=(), kind=jnp.bfloat16):
    factor_of = block_scale(stream_key, dims, shards, -0.22, 0.18) if shards else 1.0
    entries = jax.random.normal(stream_key, dims, jnp.float32) * spread * factor_of
    return jnp.minimum(jnp.maximum(entries, -reach), reach).astype(kind)


def setup_inputs(seed: int = 0) -> dict:
    arg_keys = jax.random.split(jax.random.key(seed), 7)
    features = draw_features(jax.random.fold_in(arg_keys[6], 71), 0)
    scores = centred(arg_keys[1], (ROWS,), 1.0, 6.0, ((0, 256),), jnp.float32)
    labels = draw_labels(jax.random.fold_in(arg_keys[6], 71), 0)
    query_ids = draw_query_ids(jax.random.fold_in(arg_keys[6], 71), 0)
    ranks = draw_ranks(jax.random.fold_in(arg_keys[6], 71), 0)
    leaf_ids = with_ends(ranked_ids(arg_keys[5], (ROWS,), LEAVES, 2), jax.random.fold_in(arg_keys[5], 3), 0, LEAVES - 1).astype(jnp.int32)
    return {"features": features, "scores": scores, "labels": labels, "query_ids": query_ids, "ranks": ranks, "leaf_ids": leaf_ids}


LAMBDA = 1.0
SHRINKAGE = 0.1

def discount(rank_values):
    return 1.0 / jnp.log2(1.0 + jnp.maximum(rank_values, 1.0))

def pair_block(own_rows, window):
    same_query = own_rows[0][:, None] == window[0][None, :]
    own_label = own_rows[1][:, None]
    far_label = window[1][None, :]
    counts = jnp.stack([jnp.sum(jnp.where(same_query & (far_label >= grade_level), 1.0, 0.0), axis=1) for grade_level in (1.0, 2.0, 3.0, 4.0)], axis=1)
    positions = jnp.arange(1, MAXQ + 1).astype(jnp.float32)
    prefix = jnp.sum(jnp.where(positions[None, None, :] <= counts[:, :, None], discount(positions)[None, None, :], 0.0), axis=2)
    ideal_gain = jnp.sum(prefix * jnp.array([1.0, 2.0, 4.0, 8.0], jnp.float32)[None, :], axis=1)
    inverse = 1.0 / jnp.maximum(ideal_gain, 1.0)
    gain_gap = jnp.abs(jnp.exp2(own_label) - jnp.exp2(far_label))
    disc_gap = jnp.abs(discount(own_rows[2])[:, None] - discount(window[2])[None, :])
    direction = jnp.sign(own_label - far_label)
    weight = jnp.where(same_query, gain_gap * disc_gap, 0.0)
    pair_prob = jax.nn.sigmoid(-direction * (own_rows[3][:, None] - window[3][None, :]))
    gradient = -inverse * jnp.sum(direction * weight * pair_prob, axis=1)
    hessian = inverse * jnp.sum(weight * pair_prob * (1.0 - pair_prob), axis=1)
    return (gradient, hessian)

def lambdas(padded, row_count):
    block_rows = min(512, row_count)
    zero_index = jnp.zeros((), jnp.int32)

    def one_block(block_start):
        own_rows = lax.dynamic_slice(padded, (zero_index, block_start + MAXQ), (4, block_rows))
        window = lax.dynamic_slice(padded, (zero_index, block_start), (4, block_rows + 2 * MAXQ))
        return pair_block(own_rows, window)
    starts = (jnp.arange(row_count // block_rows) * block_rows).astype(jnp.int32)
    gradients, hessians = lax.map(one_block, starts)
    return (gradients.reshape(-1), hessians.reshape(-1))

def solve_leaf(leaf_block):
    feature_count = leaf_block.shape[1]
    gram_matrix = leaf_block[:feature_count]
    weighted_sum = leaf_block[feature_count]
    moment = leaf_block[feature_count + 1]
    hess_total = leaf_block[feature_count + 2, 0]
    grad_total = leaf_block[feature_count + 2, 1]
    denominator = hess_total + LAMBDA
    system = gram_matrix + LAMBDA * jnp.eye(feature_count, dtype=jnp.float32) - weighted_sum[:, None] * weighted_sum[None, :] / denominator
    right_side = weighted_sum * grad_total / denominator - moment
    factor = jnp.linalg.cholesky(system)
    middle = lax.linalg.triangular_solve(factor, right_side[:, None], left_side=True, lower=True)
    coefficients = lax.linalg.triangular_solve(factor, middle, left_side=True, lower=True, transpose_a=True)[:, 0]
    intercept = -(grad_total + jnp.sum(weighted_sum * coefficients)) / denominator
    return (coefficients, intercept)

def reference(features, scores, labels, query_ids, ranks, leaf_ids):
    row_info = jnp.stack([(query_ids + 1).astype(jnp.float32), labels.astype(jnp.float32), ranks.astype(jnp.float32), scores])
    padded = jnp.pad(row_info, ((0, 0), (MAXQ, MAXQ)))
    gradients, hessians = lambdas(padded, row_info.shape[1])

    def leaf_terms(leaf_number):
        in_leaf = (leaf_ids == leaf_number).astype(jnp.float32)
        weighted = ((hessians * in_leaf)[:, None] * features).astype(jnp.bfloat16)
        gram_matrix = lax.dot_general(weighted.astype(jnp.float32), features.astype(jnp.float32), (((0,), (0,)), ((), ())), preferred_element_type=jnp.float32)
        weighted_sum = jnp.sum(weighted.astype(jnp.float32), axis=0)
        grad_low = (gradients * in_leaf).astype(jnp.bfloat16)
        moment = jnp.dot(grad_low.astype(jnp.float32), features.astype(jnp.float32), preferred_element_type=jnp.float32)
        total_rows = jnp.zeros((6, F), jnp.float32)
        total_rows = total_rows.at[0, 0].set(jnp.sum(hessians * in_leaf)).at[0, 1].set(jnp.sum(gradients * in_leaf))
        return jnp.concatenate([gram_matrix, weighted_sum[None, :], moment[None, :], total_rows], axis=0)
    all_terms = lax.map(leaf_terms, jnp.arange(LEAVES).astype(jnp.int32))
    coefficients, intercepts = jax.vmap(solve_leaf)(all_terms)
    per_leaf = jnp.dot(features.astype(jnp.float32), coefficients.T, precision=lax.Precision.HIGHEST) + intercepts[None, :]
    chosen = leaf_ids[:, None] == jnp.arange(LEAVES).astype(jnp.int32)[None, :]
    tree_output = jnp.sum(jnp.where(chosen, per_leaf, 0.0), axis=1)
    new_scores = scores + SHRINKAGE * tree_output
    return (gradients, tree_output, new_scores)
```

```python
import jax
import jax.numpy as jnp
from jax import lax
from jax.experimental import pallas as pl
from jax.experimental.pallas import tpu as pltpu
from jax.sharding import Mesh
from jax.sharding import PartitionSpec as P

LEAVES = 16
MAXQ = 128
ROWS = 1024
BLOCKS = ROWS // MAXQ
F = 256
HALF = 128
LEAF_ROWS = 272
DOC_LEAF = ("doc", "leaf_0", "leaf_1", "leaf_2")
LEAF = ("leaf_0", "leaf_1", "leaf_2")
LAMBDA = 1.0
SHRINKAGE = 0.1
F32 = jnp.float32
BF16 = jnp.bfloat16
NT = (((1,), (1,)), ((), ()))
VMEM = pl.BlockSpec(memory_space=pltpu.VMEM)


def iota(shape, dim):
    return lax.broadcasted_iota(jnp.int32, shape, dim)


def discount(rank_values):
    return 1.0 / jnp.log2(1.0 + jnp.maximum(rank_values, 1.0))


def stacked(rows):
    width = rows[0].shape[1]
    sub = iota((8, width), 0)
    out = jnp.zeros((8, width), F32)
    for k, row in enumerate(rows):
        out = jnp.where(sub == k, jnp.broadcast_to(row, (8, width)), out)
    return out


def pair_sums(own, far_cols, far_ge):
    query, gain, disc, score = own
    far_query, far_gain, far_disc, far_score = far_cols
    same = far_query == query
    gain_gap = gain - far_gain
    score_gap = score - far_score
    signed = jnp.where(same, gain_gap * jnp.abs(disc - far_disc), 0.0)
    prob = 1.0 / (1.0 + jnp.exp(jnp.where(gain_gap >= 0.0, score_gap, -score_gap)))
    pull = signed * prob
    grad = jnp.sum(pull, axis=0, keepdims=True)
    hess = jnp.sum(jnp.abs(pull) * (1.0 - prob), axis=0, keepdims=True)
    mates = jnp.where(same, 1.0, 0.0).astype(BF16)
    counts = jnp.dot(far_ge, mates, preferred_element_type=F32)
    return grad, hess, counts


def far_block(query, label, rank, score):
    gain = jnp.exp2(label)
    disc = discount(rank)
    turned = stacked([query, gain, disc, score]).T
    cols = [jnp.broadcast_to(turned[:, c : c + 1], (MAXQ, MAXQ)) for c in range(4)]
    level = (iota((16, MAXQ), 0) + 1).astype(F32)
    at_least = jnp.where(jnp.broadcast_to(label, (16, MAXQ)) >= level, 1.0, 0.0).astype(BF16)
    return cols, at_least


def lambdas(query_ref, label_ref, rank_ref, score_ref, halo):
    query = query_ref[...].astype(F32)
    label = label_ref[...].astype(F32)
    rank = rank_ref[...].astype(F32)
    score = score_ref[...]
    gain = jnp.exp2(label)
    disc = discount(rank)
    own = [[x[k : k + 1, :] for x in (query, gain, disc, score)] for k in range(BLOCKS)]
    sums = [None] * BLOCKS

    def meet(k, far):
        new = pair_sums(own[k], *far)
        sums[k] = new if sums[k] is None else tuple(a + b for a, b in zip(sums[k], new))

    for j in range(BLOCKS):
        far = far_block(*[x[j : j + 1, :] for x in (query, label, rank, score)])
        for k in (j - 1, j, j + 1):
            if 0 <= k < BLOCKS:
                meet(k, far)
    before, after = halo()
    meet(0, far_block(*[before[c : c + 1, :] for c in range(4)]))
    meet(BLOCKS - 1, far_block(*[after[c : c + 1, :] for c in range(4)]))

    position = (iota((MAXQ, MAXQ), 0) + 1).astype(F32)
    disc_at = discount(position)
    grads, hess = [], []
    for k in range(BLOCKS):
        pull, push, counts = sums[k]
        ideal = jnp.zeros((1, MAXQ), F32)
        for level in range(4):
            inside = jnp.where(position <= counts[level : level + 1, :], disc_at, 0.0)
            ideal = ideal + float(2**level) * jnp.sum(inside, axis=0, keepdims=True)
        inverse = 1.0 / jnp.maximum(ideal, 1.0)
        grads.append(-inverse * pull)
        hess.append(inverse * push)
    return grads, hess


def leaf_inputs(features_ref, leaf_ref, grads, hess, weighted_ref, in_leaf_ref, sums_ref):
    leaf = leaf_ref[...]
    grad_low = []
    h_lanes = jnp.zeros((LEAVES, MAXQ), F32)
    g_lanes = jnp.zeros((LEAVES, MAXQ), F32)
    for k in range(BLOCKS):
        rows = slice(MAXQ * k, MAXQ * (k + 1))
        turned = features_ref[rows, :].astype(F32).T
        weighted_ref[:, rows] = (turned * hess[k]).astype(BF16)
        in_leaf = jnp.where(
            jnp.broadcast_to(leaf[k : k + 1, :], (LEAVES, MAXQ)) == iota((LEAVES, MAXQ), 0),
            1.0,
            0.0,
        )
        in_leaf_ref[:, rows] = in_leaf
        h_lanes = h_lanes + in_leaf * hess[k]
        g_lanes = g_lanes + in_leaf * grads[k]
        grad_low.append((in_leaf * grads[k]).astype(BF16))
    moment = jnp.dot(
        jnp.concatenate(grad_low, axis=1), features_ref[...], preferred_element_type=F32
    )
    hsum = lax.dot_general(
        in_leaf_ref[...].astype(BF16), weighted_ref[...], NT, preferred_element_type=F32
    )
    wide = (LEAVES, MAXQ)
    sums_ref[0] = hsum[:, :HALF]
    sums_ref[1] = hsum[:, HALF:]
    sums_ref[2] = moment[:, :HALF]
    sums_ref[3] = moment[:, HALF:]
    sums_ref[4] = jnp.broadcast_to(jnp.sum(h_lanes, axis=1, keepdims=True), wide)
    sums_ref[5] = jnp.broadcast_to(jnp.sum(g_lanes, axis=1, keepdims=True), wide)


def leaf_gram(number, features_ref, weighted_ref, in_leaf_ref):
    mask = jnp.broadcast_to(in_leaf_ref[pl.ds(number, 1), :], (16, ROWS)).astype(BF16)
    own = (weighted_ref[...].reshape(16, 16, ROWS) * mask[None]).reshape(F, ROWS)
    return jnp.dot(own, features_ref[...], preferred_element_type=F32)


def packed_leaf(gram, number, sums_ref):
    row = iota((HALF, HALF), 0)
    col = iota((HALF, HALF), 1)
    last = gram[HALF:, HALF:]
    mixed = jnp.where(col <= row, gram[:HALF, :HALF], last)
    diag = jnp.sum(jnp.where(col == row, last, 0.0), axis=0, keepdims=True)
    small = [sums_ref[k, pl.ds(number, 1), :] for k in range(6)]
    extra = stacked(small + [diag])
    first = jnp.concatenate(
        [mixed[:64], extra, mixed[64:], jnp.zeros((8, HALF), F32)], axis=0
    )
    return first, gram[HALF:, :HALF]


def dotted(a, b, dims=(((1,), (0,)), ((), ()))):
    return lax.dot_general(
        a, b, dims, precision=lax.Precision.HIGHEST, preferred_element_type=F32
    )


def small_inverse(d):
    p = len(d)
    if p == 1:
        return [[1.0 / d[0][0]]]
    if p == 2:
        a, b, c = d[0][0], d[0][1], d[1][1]
        r = 1.0 / (a * c - b * b)
        n = -b * r
        return [[c * r, n], [n, a * r]]
    h = p // 2

    def dot(xs, ys):
        total = xs[0] * ys[0]
        for x, y in zip(xs[1:], ys[1:]):
            total = total + x * y
        return total

    first = small_inverse([line[:h] for line in d[:h]])
    side = [line[h:] for line in d[:h]]
    u = [[dot(first[i], [side[m][j] for m in range(h)]) for j in range(h)] for i in range(h)]
    rest = [[None] * h for _ in range(h)]
    for i in range(h):
        for j in range(i, h):
            rest[i][j] = rest[j][i] = d[h + i][h + j] - dot(
                [side[m][i] for m in range(h)], [u[m][j] for m in range(h)]
            )
    last = small_inverse(rest)
    out = [[None] * p for _ in range(p)]
    for i in range(h):
        for j in range(h):
            out[h + i][h + j] = last[i][j]
            out[i][h + j] = out[h + j][i] = -dot(u[i], [last[m][j] for m in range(h)])
    for i in range(h):
        for j in range(i, h):
            out[i][j] = out[j][i] = first[i][j] - dot(
                [out[i][h + m] for m in range(h)], [u[j][m] for m in range(h)]
            )
    return out


def spd_inverse(m, p):
    n = m.shape[0]
    lane = iota((8, n), 1)
    sub = iota((8, n), 0)
    for k in range(0, n, p):
        top = k // 8 * 8
        cols = [jnp.broadcast_to(m[:, k + b : k + b + 1], m.shape) for b in range(p)]
        rows = [jnp.broadcast_to(m[k + a : k + a + 1, :], (8, n)) for a in range(p)]
        d = [[None] * p for _ in range(p)]
        for a in range(p):
            for b in range(a, p):
                d[a][b] = d[b][a] = jnp.broadcast_to(cols[b][k + a : k + a + 1, :], (8, n))
        v = small_inverse(d)
        scaled = []
        for a in range(p):
            r = v[a][0] * rows[0]
            for b in range(1, p):
                r = r + v[a][b] * rows[b]
            for b in range(p):
                r = jnp.where(lane == k + b, v[a][b], r)
            scaled.append(r)
        pivot = (lane >= k) & (lane < k + p)
        tiles = []
        for t in range(0, n, 8):
            tile = jnp.where(pivot, 0.0, m[t : t + 8, :])
            for a in range(p):
                tile = tile - cols[a][t : t + 8, :] * scaled[a]
            if t == top:
                for a in range(p):
                    tile = jnp.where(sub == k - top + a, scaled[a], tile)
            tiles.append(tile)
        m = jnp.concatenate(tiles, axis=0)
    return m


def solved(mixed, extra, low):
    row = iota((HALF, HALF), 0)
    col = iota((HALF, HALF), 1)
    turned = mixed.T
    hsum = [extra[0:1, :], extra[1:2, :]]
    moment = [extra[2:3, :], extra[3:4, :]]
    htotal, gtotal, diag = extra[4:5, :], extra[5:6, :], extra[6:7, :]
    share = 1.0 / (htotal + LAMBDA)
    scaled = [h * share for h in hsum]
    across = stacked(hsum).T
    over = [jnp.broadcast_to(across[:, k : k + 1], (HALF, HALF)) for k in range(2)]
    unit = jnp.where(row == col, LAMBDA, 0.0)
    a11 = jnp.where(col <= row, mixed, turned) + unit - over[0] * scaled[0]
    a21 = low - over[1] * scaled[0]
    a22 = jnp.where(col > row, mixed, jnp.where(col < row, turned, diag))
    a22 = a22 + unit - over[1] * scaled[1]
    side = [scaled[k] * gtotal - moment[k] for k in range(2)]
    inv1 = spd_inverse(a11, 8)
    z = dotted(a21, inv1)
    inv2 = spd_inverse(a22 - dotted(z, a21, NT), 8)
    b1 = jnp.broadcast_to(side[0], (8, HALF))
    b2 = jnp.broadcast_to(side[1], (8, HALF))
    w2 = dotted(b2 - dotted(b1, z, NT), inv2)
    w1 = dotted(b1, inv1) - dotted(w2, z)
    total = jnp.sum(hsum[0] * w1 + hsum[1] * w2, axis=1, keepdims=True)
    c = -(gtotal + total) * share
    return stacked([w1[0:1], w2[0:1], c[0:1]])


def leaf_output(features_ref, leaf_ref, score_ref, weights, intercepts, tree_ref, new_ref):
    high = weights.astype(BF16)
    left = weights - high.astype(F32)
    mid = left.astype(BF16)
    low = (left - mid.astype(F32)).astype(BF16)
    parts = jnp.concatenate([high, mid, low], axis=0)
    sums = lax.dot_general(parts, features_ref[...], NT, preferred_element_type=F32)
    per_leaf = sums[:16] + sums[16:32] + sums[32:48]
    leaf = leaf_ref[...]
    for k in range(BLOCKS):
        rows = slice(MAXQ * k, MAXQ * (k + 1))
        own = jnp.broadcast_to(leaf[k : k + 1, :], (LEAVES, MAXQ)) == iota((LEAVES, MAXQ), 0)
        tree = jnp.sum(
            jnp.where(own, per_leaf[:, rows] + intercepts, 0.0), axis=0, keepdims=True
        )
        tree_ref[k : k + 1, :] = tree
        new_ref[k : k + 1, :] = score_ref[k : k + 1, :] + SHRINKAGE * tree


def terms_kernel(
    features, score, label, query, rank, leaf, before, after, grad_out, packed, weighted, in_leaf, sums
):
    grads, hess = lambdas(query, label, rank, score, lambda: (before[...], after[...]))
    for k in range(BLOCKS):
        grad_out[k : k + 1, :] = grads[k]
    leaf_inputs(features, leaf, grads, hess, weighted, in_leaf, sums)

    def one(number, carry):
        first, second = packed_leaf(leaf_gram(number, features, weighted, in_leaf), number, sums)
        packed[number, :144, :] = first
        packed[number, 144:, :] = second
        return carry

    lax.fori_loop(0, LEAVES, one, 0)


def solve_kernel(packed, out):
    block = packed[...]
    mixed = jnp.concatenate([block[:64], block[72:136]], axis=0)
    out[...] = solved(mixed, block[64:72], block[144:])


def output_kernel(features, leaf, score, coefs, tree, new):
    all_rows = coefs[...]
    weights = jnp.concatenate([all_rows[0], all_rows[1]], axis=1)
    leaf_output(features, leaf, score, weights, all_rows[2], tree, new)


def passed_along(value, axis, by):
    devices = lax.axis_size(axis)
    return lax.ppermute(value, axis, [(i, (i + by) % devices) for i in range(devices)])


def body(features, scores, labels, query_ids, ranks, leaf_ids):
    lines = [x.reshape(BLOCKS, MAXQ) for x in (scores, labels, query_ids, ranks, leaf_ids)]
    score, label, query, rank, leaf = lines
    info = jnp.stack([x.astype(F32) for x in (query, label, rank, score)])
    index = lax.axis_index(DOC_LEAF)
    before = passed_along(info[:, BLOCKS - 1], DOC_LEAF, 1)
    after = passed_along(info[:, 0], DOC_LEAF, -1)
    none = jnp.full((1, MAXQ), -1.0, F32)
    before = jnp.where((index == 0) & (jnp.arange(4)[:, None] == 0), none, before)
    after = jnp.where(
        (index == lax.axis_size(DOC_LEAF) - 1) & (jnp.arange(4)[:, None] == 0), none, after
    )
    grads, packed = pl.pallas_call(
        terms_kernel,
        out_shape=[
            jax.ShapeDtypeStruct((BLOCKS, MAXQ), F32),
            jax.ShapeDtypeStruct((LEAVES, LEAF_ROWS, HALF), F32),
        ],
        in_specs=[VMEM] * 8,
        out_specs=[VMEM] * 2,
        scratch_shapes=[
            pltpu.VMEM((F, ROWS), BF16),
            pltpu.VMEM((LEAVES, ROWS), F32),
            pltpu.VMEM((6, LEAVES, MAXQ), F32),
        ],
    )(features, score, label, query, rank, leaf, before, after)
    part = lax.psum_scatter(packed, LEAF, scatter_dimension=0, tiled=False)
    total = lax.psum(part, "doc")
    coefs = pl.pallas_call(
        solve_kernel,
        out_shape=jax.ShapeDtypeStruct((8, HALF), F32),
        in_specs=[VMEM],
        out_specs=VMEM,
    )(total)
    gathered = lax.all_gather(coefs, LEAF, axis=1)
    tree, new = pl.pallas_call(
        output_kernel,
        out_shape=[jax.ShapeDtypeStruct((BLOCKS, MAXQ), F32)] * 2,
        in_specs=[VMEM] * 4,
        out_specs=[VMEM] * 2,
    )(features, leaf, score, gathered)
    return grads.reshape(ROWS), tree.reshape(ROWS), new.reshape(ROWS)


def solution(mesh):
    torus = Mesh(
        mesh.devices.reshape(mesh.shape["doc"], 4, 2, 2), ("doc", "leaf_0", "leaf_1", "leaf_2")
    )
    spec = P(DOC_LEAF)
    return jax.shard_map(
        body,
        mesh=torus,
        in_specs=(P(DOC_LEAF, None), spec, spec, spec, spec, spec),
        out_specs=(spec, spec, spec),
        check_vma=False,
    )
```

```python
import jax
import jax.numpy as jnp
from jax import lax
from jax.experimental import pallas as pl
from jax.experimental.pallas import tpu as pltpu
from jax.sharding import Mesh
from jax.sharding import PartitionSpec as P

LEAVES = 16
MAXQ = 128
ROWS = 1024
BLOCKS = ROWS // MAXQ
F = 256
HALF = 128
LEAF_ROWS = 272
AXES = ("z", "y_lo", "x", "y_hi", "core")
MESH = pl.DeviceIdType.MESH
PIVOTS = 4
LAMBDA = 1.0
SHRINKAGE = 0.1
F32 = jnp.float32
BF16 = jnp.bfloat16
NT = (((1,), (1,)), ((), ()))
VMEM = pl.BlockSpec(memory_space=pltpu.VMEM)


def iota(shape, dim):
    return lax.broadcasted_iota(jnp.int32, shape, dim)


def discount(rank_values):
    return 1.0 / jnp.log2(1.0 + jnp.maximum(rank_values, 1.0))


def stacked(rows):
    width = rows[0].shape[1]
    sub = iota((8, width), 0)
    out = jnp.zeros((8, width), F32)
    for k, row in enumerate(rows):
        out = jnp.where(sub == k, jnp.broadcast_to(row, (8, width)), out)
    return out


def pair_sums(own, far_cols, far_ge):
    query, gain, disc, score = own
    far_query, far_gain, far_disc, far_score = far_cols
    same = far_query == query
    gain_gap = gain - far_gain
    score_gap = score - far_score
    signed = jnp.where(same, gain_gap * jnp.abs(disc - far_disc), 0.0)
    prob = 1.0 / (1.0 + jnp.exp(jnp.where(gain_gap >= 0.0, score_gap, -score_gap)))
    pull = signed * prob
    grad = jnp.sum(pull, axis=0, keepdims=True)
    hess = jnp.sum(jnp.abs(pull) * (1.0 - prob), axis=0, keepdims=True)
    mates = jnp.where(same, 1.0, 0.0).astype(BF16)
    counts = jnp.dot(far_ge, mates, preferred_element_type=F32)
    return grad, hess, counts


def far_block(query, label, rank, score):
    gain = jnp.exp2(label)
    disc = discount(rank)
    turned = stacked([query, gain, disc, score]).T
    cols = [jnp.broadcast_to(turned[:, c : c + 1], (MAXQ, MAXQ)) for c in range(4)]
    level = (iota((16, MAXQ), 0) + 1).astype(F32)
    at_least = jnp.where(jnp.broadcast_to(label, (16, MAXQ)) >= level, 1.0, 0.0).astype(BF16)
    return cols, at_least


def own_rows(query_ref, label_ref, rank_ref, score_ref):
    query = query_ref[...].astype(F32)
    label = label_ref[...].astype(F32)
    rank = rank_ref[...].astype(F32)
    return query, label, rank, score_ref[...]


def meet(own, sums, k, far):
    new = pair_sums([x[k : k + 1, :] for x in own], *far)
    sums[k] = new if sums[k] is None else tuple(a + b for a, b in zip(sums[k], new))


def lambdas_within(rows):
    query, label, rank, score = rows
    own = (query, jnp.exp2(label), discount(rank), score)
    sums = [None] * BLOCKS
    for j in range(BLOCKS):
        far = far_block(*[x[j : j + 1, :] for x in rows])
        for k in (j - 1, j, j + 1):
            if 0 <= k < BLOCKS:
                meet(own, sums, k, far)
    return own, sums


def lambdas_across(own, sums, before, after):
    meet(own, sums, 0, far_block(*[before[c : c + 1, :] for c in range(4)]))
    meet(own, sums, BLOCKS - 1, far_block(*[after[c : c + 1, :] for c in range(4)]))


def normalized(sums):
    position = (iota((MAXQ, MAXQ), 0) + 1).astype(F32)
    disc_at = discount(position)
    grads, hess = [], []
    for pull, push, counts in sums:
        ideal = jnp.zeros((1, MAXQ), F32)
        for level in range(4):
            inside = jnp.where(position <= counts[level : level + 1, :], disc_at, 0.0)
            ideal = ideal + float(2**level) * jnp.sum(inside, axis=0, keepdims=True)
        inverse = 1.0 / jnp.maximum(ideal, 1.0)
        grads.append(-inverse * pull)
        hess.append(inverse * push)
    return grads, hess


def leaf_inputs(features_ref, leaf_ref, grads, hess, weighted_ref, in_leaf_ref, sums_ref):
    leaf = leaf_ref[...]
    grad_low = []
    h_lanes = jnp.zeros((LEAVES, MAXQ), F32)
    g_lanes = jnp.zeros((LEAVES, MAXQ), F32)
    for k in range(BLOCKS):
        rows = slice(MAXQ * k, MAXQ * (k + 1))
        turned = features_ref[rows, :].astype(F32).T
        weighted_ref[:, rows] = (turned * hess[k]).astype(BF16)
        in_leaf = jnp.where(
            jnp.broadcast_to(leaf[k : k + 1, :], (LEAVES, MAXQ)) == iota((LEAVES, MAXQ), 0),
            1.0,
            0.0,
        )
        in_leaf_ref[:, rows] = in_leaf
        h_lanes = h_lanes + in_leaf * hess[k]
        g_lanes = g_lanes + in_leaf * grads[k]
        grad_low.append((in_leaf * grads[k]).astype(BF16))
    moment = jnp.dot(
        jnp.concatenate(grad_low, axis=1), features_ref[...], preferred_element_type=F32
    )
    hsum = lax.dot_general(
        in_leaf_ref[...].astype(BF16), weighted_ref[...], NT, preferred_element_type=F32
    )
    wide = (LEAVES, MAXQ)
    sums_ref[0] = hsum[:, :HALF]
    sums_ref[1] = hsum[:, HALF:]
    sums_ref[2] = moment[:, :HALF]
    sums_ref[3] = moment[:, HALF:]
    sums_ref[4] = jnp.broadcast_to(jnp.sum(h_lanes, axis=1, keepdims=True), wide)
    sums_ref[5] = jnp.broadcast_to(jnp.sum(g_lanes, axis=1, keepdims=True), wide)


def leaf_gram(number, features_ref, weighted_ref, in_leaf_ref):
    mask = jnp.broadcast_to(in_leaf_ref[pl.ds(number, 1), :], (16, ROWS)).astype(BF16)
    own = (weighted_ref[...].reshape(16, 16, ROWS) * mask[None]).reshape(F, ROWS)
    return jnp.dot(own, features_ref[...], preferred_element_type=F32)


def packed_leaf(gram, number, sums_ref):
    row = iota((HALF, HALF), 0)
    col = iota((HALF, HALF), 1)
    last = gram[HALF:, HALF:]
    mixed = jnp.where(col <= row, gram[:HALF, :HALF], last)
    diag = jnp.sum(jnp.where(col == row, last, 0.0), axis=0, keepdims=True)
    small = [sums_ref[k, pl.ds(number, 1), :] for k in range(6)]
    extra = stacked(small + [diag])
    first = jnp.concatenate(
        [mixed[:64], extra, mixed[64:], jnp.zeros((8, HALF), F32)], axis=0
    )
    return first, gram[HALF:, :HALF]


def dotted(a, b, dims=(((1,), (0,)), ((), ()))):
    return lax.dot_general(
        a, b, dims, precision=lax.Precision.HIGHEST, preferred_element_type=F32
    )


def small_inverse(d):
    p = len(d)
    if p == 1:
        return [[1.0 / d[0][0]]]
    if p == 2:
        a, b, c = d[0][0], d[0][1], d[1][1]
        r = 1.0 / (a * c - b * b)
        n = -b * r
        return [[c * r, n], [n, a * r]]
    h = p // 2

    def dot(xs, ys):
        total = xs[0] * ys[0]
        for x, y in zip(xs[1:], ys[1:]):
            total = total + x * y
        return total

    first = small_inverse([line[:h] for line in d[:h]])
    side = [line[h:] for line in d[:h]]
    u = [[dot(first[i], [side[m][j] for m in range(h)]) for j in range(h)] for i in range(h)]
    rest = [[None] * h for _ in range(h)]
    for i in range(h):
        for j in range(i, h):
            rest[i][j] = rest[j][i] = d[h + i][h + j] - dot(
                [side[m][i] for m in range(h)], [u[m][j] for m in range(h)]
            )
    last = small_inverse(rest)
    out = [[None] * p for _ in range(p)]
    for i in range(h):
        for j in range(h):
            out[h + i][h + j] = last[i][j]
            out[i][h + j] = out[h + j][i] = -dot(u[i], [last[m][j] for m in range(h)])
    for i in range(h):
        for j in range(i, h):
            out[i][j] = out[j][i] = first[i][j] - dot(
                [out[i][h + m] for m in range(h)], [u[j][m] for m in range(h)]
            )
    return out


def spd_inverse(m, p):
    n = m.shape[0]
    lane = iota((8, n), 1)
    sub = iota((8, n), 0)
    for k in range(0, n, p):
        top = k // 8 * 8
        cols = [jnp.broadcast_to(m[:, k + b : k + b + 1], m.shape) for b in range(p)]
        rows = [jnp.broadcast_to(m[k + a : k + a + 1, :], (8, n)) for a in range(p)]
        d = [[None] * p for _ in range(p)]
        for a in range(p):
            for b in range(a, p):
                d[a][b] = d[b][a] = jnp.broadcast_to(cols[b][k + a : k + a + 1, :], (8, n))
        v = small_inverse(d)
        scaled = []
        for a in range(p):
            r = v[a][0] * rows[0]
            for b in range(1, p):
                r = r + v[a][b] * rows[b]
            for b in range(p):
                r = jnp.where(lane == k + b, v[a][b], r)
            scaled.append(r)
        pivot = (lane >= k) & (lane < k + p)
        whole = jnp.where(jnp.broadcast_to(pivot[:1], m.shape), 0.0, m)
        for a in range(p):
            whole = whole - cols[a] * jnp.broadcast_to(scaled[a][:1], m.shape)
        tile = whole[top : top + 8]
        for a in range(p):
            tile = jnp.where(sub == k - top + a, scaled[a], tile)
        parts = [whole[:top]] if top else []
        parts += [tile]
        parts += [whole[top + 8 :]] if top + 8 < n else []
        m = jnp.concatenate(parts, axis=0)
    return m


def solved(mixed, extra, low):
    row = iota((HALF, HALF), 0)
    col = iota((HALF, HALF), 1)
    turned = mixed.T
    hsum = [extra[0:1, :], extra[1:2, :]]
    moment = [extra[2:3, :], extra[3:4, :]]
    htotal, gtotal, diag = extra[4:5, :], extra[5:6, :], extra[6:7, :]
    share = 1.0 / (htotal + LAMBDA)
    scaled = [h * share for h in hsum]
    across = stacked(hsum).T
    over = [jnp.broadcast_to(across[:, k : k + 1], (HALF, HALF)) for k in range(2)]
    unit = jnp.where(row == col, LAMBDA, 0.0)
    a11 = jnp.where(col <= row, mixed, turned) + unit - over[0] * scaled[0]
    a21 = low - over[1] * scaled[0]
    a22 = jnp.where(col > row, mixed, jnp.where(col < row, turned, diag))
    a22 = a22 + unit - over[1] * scaled[1]
    side = [scaled[k] * gtotal - moment[k] for k in range(2)]
    inv1 = spd_inverse(a11, PIVOTS)
    z = dotted(a21, inv1)
    inv2 = spd_inverse(a22 - dotted(z, a21, NT), PIVOTS)
    b1 = jnp.broadcast_to(side[0], (8, HALF))
    b2 = jnp.broadcast_to(side[1], (8, HALF))
    w2 = dotted(b2 - dotted(b1, z, NT), inv2)
    w1 = dotted(b1, inv1) - dotted(w2, z)
    total = jnp.sum(hsum[0] * w1 + hsum[1] * w2, axis=1, keepdims=True)
    c = -(gtotal + total) * share
    return stacked([w1[0:1], w2[0:1], c[0:1]])


def leaf_output(features_ref, leaf_ref, score_ref, weights, intercepts, tree_ref, new_ref):
    high = weights.astype(BF16)
    left = weights - high.astype(F32)
    mid = left.astype(BF16)
    low = (left - mid.astype(F32)).astype(BF16)
    parts = jnp.concatenate([high, mid, low], axis=0)
    sums = lax.dot_general(parts, features_ref[...], NT, preferred_element_type=F32)
    per_leaf = sums[:16] + sums[16:32] + sums[32:48]
    leaf = leaf_ref[...]
    for k in range(BLOCKS):
        rows = slice(MAXQ * k, MAXQ * (k + 1))
        own = jnp.broadcast_to(leaf[k : k + 1, :], (LEAVES, MAXQ)) == iota((LEAVES, MAXQ), 0)
        tree = jnp.sum(
            jnp.where(own, per_leaf[:, rows] + intercepts, 0.0), axis=0, keepdims=True
        )
        tree_ref[k : k + 1, :] = tree
        new_ref[k : k + 1, :] = score_ref[k : k + 1, :] + SHRINKAGE * tree


def position():
    z, y_lo, x, y_hi, core = [lax.axis_index(a) for a in AXES]
    return z, 2 * y_hi + y_lo, x, core


def device(z, y, x, core):
    return (z, lax.rem(y, 2), x, lax.div(y, 2), core)


def neighbour(by):
    index = jnp.int32(0)
    total = 1
    for a in AXES:
        index = index * lax.axis_size(a) + lax.axis_index(a)
        total *= lax.axis_size(a)
    index = lax.rem(index + by + total, total)
    place = []
    for a in reversed(AXES):
        place.append(lax.rem(index, lax.axis_size(a)))
        index = lax.div(index, lax.axis_size(a))
    return tuple(reversed(place))


def ahead(value, by, size):
    return lax.rem(value + by, size)


def level_kernel(
    features, score, label, query, rank, leaf,
    out,
    weighted, in_leaf, sums_ref,
    edge, before, after,
    pair_out, pair_in,
    first_sum, second_sum, first_in, second_in,
    first_part, second_part, first_in2, second_in2,
    slab, slab_in, final, first_all, second_all, coef, coefs,
    halo_send, halo_recv, pair_send, pair_recv,
    p1x_send, p1x_recv, p1y_send, p1y_recv,
    p2x_send, p2x_recv, p2y_send, p2y_recv,
    z_send, z_recv, gx_send, gx_recv, gy_send, gy_recv,
    w_send, w_recv,
):
    z, y, x, core = position()
    depth = lax.axis_size("z")
    y_lo, x_lo = lax.rem(y, 2), lax.rem(x, 2)
    y_hi, x_hi = lax.div(y, 2), lax.div(x, 2)
    y_pair, x_pair = y + 1 - 2 * y_lo, x + 1 - 2 * x_lo
    other = 1 - core
    solver = x_lo == y_lo
    in_plane = [
        (dx, dy, dc) for dx in (2, 1, 3, 0) for dy in (2, 1, 3, 0) for dc in (1, 0) if dx or dy or dc
    ]

    def plane(dx, dy, dc):
        return device(z, ahead(y, dy, 4), ahead(x, dx, 4), ahead(core, dc, 2))

    barrier = pltpu.get_barrier_semaphore()
    partners = [neighbour(1), neighbour(-1)] + [plane(*d) for d in in_plane]
    for d in range(1, depth):
        at = ahead(z, d, depth)
        partners += [device(at, y, x, core), device(at, y_pair, x, core), device(at, y, x_pair, core)]
    for partner in partners:
        pl.semaphore_signal(barrier, inc=1, device_id=partner, device_id_type=MESH)

    def remote(src, dst, send, recv, to):
        return pltpu.make_async_remote_copy(
            src_ref=src, dst_ref=dst, send_sem=send, recv_sem=recv, device_id=to, device_id_type=MESH
        )

    rows = own_rows(query, label, rank, score)
    edge[0] = stacked([r[BLOCKS - 1 : BLOCKS, :] for r in rows])
    edge[1] = stacked([r[0:1, :] for r in rows])
    own, sums = lambdas_within(rows)
    pl.semaphore_wait(barrier, len(partners))

    later, earlier = neighbour(1), neighbour(-1)
    to_later = remote(edge.at[0], before, halo_send.at[0], halo_recv.at[0], later)
    to_earlier = remote(edge.at[1], after, halo_send.at[1], halo_recv.at[1], earlier)
    to_later.start()
    to_earlier.start()
    to_later.wait()
    to_earlier.wait()
    first_device = (z == 0) & (y_lo == 0) & (x == 0) & (y_hi == 0) & (core == 0)
    last_device = (z == depth - 1) & (y_lo == 1) & (x == 3) & (y_hi == 1) & (core == 1)
    top = iota((8, MAXQ), 0) == 0
    was = jnp.where(top & first_device, -1.0, before[...])
    will = jnp.where(top & last_device, -1.0, after[...])
    lambdas_across(own, sums, was, will)
    grads, hess = normalized(sums)
    for k in range(BLOCKS):
        out[0, k : k + 1, :] = grads[k]
    leaf_inputs(features, leaf, grads, hess, weighted, in_leaf, sums_ref)

    def turn(t):
        return lax.rem(2 * (x + 1) + t, 8)

    def pair_copy(j):
        return remote(
            pair_out.at[j], pair_in.at[j], pair_send.at[j], pair_recv.at[j], plane(0, 0, 1)
        )

    def for_other(t, carry):
        j = turn(t)
        number = 8 * other + j
        first, second = packed_leaf(leaf_gram(number, features, weighted, in_leaf), number, sums_ref)
        pair_out[j, :144, :] = first
        pair_out[j, 144:, :] = second
        pair_copy(j).start()
        return carry

    lax.fori_loop(0, 8, for_other, 0)

    def p1x_copy(t):
        j, d = turn(t), lax.div(t, 2) + 1
        return remote(
            first_sum.at[j],
            first_in.at[d - 1, lax.rem(t, 2)],
            p1x_send.at[j],
            p1x_recv.at[d - 1, lax.rem(t, 2)],
            device(z, y, ahead(x, d, 4), core),
        )

    def row_of(j):
        return 2 * lax.rem(j, 2) + lax.rem(lax.div(j, 2), 2)

    def p1y_copy(j):
        d = lax.rem(row_of(j) - y + 4, 4)
        return remote(
            second_sum.at[j],
            second_in.at[lax.rem(d + 3, 4), lax.div(j, 4)],
            p1y_send.at[j],
            p1y_recv.at[lax.rem(d + 3, 4), lax.div(j, 4)],
            device(z, row_of(j), x, core),
        )

    def for_own(t, carry):
        j = turn(t)
        number = 8 * core + j
        first, second = packed_leaf(leaf_gram(number, features, weighted, in_leaf), number, sums_ref)
        pair_copy(j).wait_recv()
        first_sum[j] = first + pair_in[j, :144, :]
        second_sum[j] = second + pair_in[j, 144:, :]

        @pl.when(t < 6)
        def _():
            p1x_copy(t).start()

        @pl.when(row_of(j) != y)
        def _():
            p1y_copy(j).start()

        return carry

    lax.fori_loop(0, 8, for_own, 0)

    for h in range(2):
        for d in range(1, 4):
            p1x_copy(2 * (d - 1) + h).wait_recv()
        total = first_sum[2 * x + h] + first_in[0, h] + first_in[1, h] + first_in[2, h]
        first_part[2 * h] = total[:72]
        first_part[2 * h + 1] = total[72:]

    def p2x_copy(d):
        at = ahead(y, d, 4)
        return remote(
            first_part.at[at], first_in2.at[d - 1], p2x_send.at[d - 1], p2x_recv.at[d - 1],
            device(z, at, x, core),
        )

    def p2y_copy(d):
        at = ahead(x, d, 4)
        return remote(
            second_part.at[at], second_in2.at[d - 1], p2y_send.at[d - 1], p2y_recv.at[d - 1],
            device(z, y, at, core),
        )

    for d in (2, 1, 3):
        p2x_copy(d).start()
    for u in range(2):
        for d in range(1, 4):
            remote(
                second_sum.at[0], second_in.at[d - 1, u], p1y_send.at[0], p1y_recv.at[d - 1, u],
                device(z, ahead(y, d, 4), x, core),
            ).wait_recv()
        j = 4 * u + 2 * y_lo + y_hi
        total = second_sum[j] + second_in[0, u] + second_in[1, u] + second_in[2, u]
        second_part[2 * u] = total[:64]
        second_part[2 * u + 1] = total[64:]
    for d in (2, 1, 3):
        p2y_copy(d).start()

    for d in range(1, 4):
        p2x_copy(d).wait_recv()
    total = first_part[y] + first_in2[0] + first_in2[1] + first_in2[2]
    slab[:, 0:8, :] = total[:64].reshape(8, 8, HALF)
    slab[:, 8:16, :] = jnp.broadcast_to(total[64:][None], (8, 8, HALF))
    for d in range(1, 4):
        p2y_copy(d).wait_recv()
    total = second_part[x] + second_in2[0] + second_in2[1] + second_in2[2]
    slab[:, 16:24, :] = total.reshape(8, 8, HALF)

    def z_copy(d):
        at = ahead(z, d, depth)
        return remote(
            slab.at[at], slab_in.at[d - 1], z_send.at[d - 1], z_recv.at[d - 1],
            device(at, y, x, core),
        )

    order = (4, 3, 5, 2, 6, 1, 7)
    for d in order:
        z_copy(d).start()
    for d in order:
        z_copy(d).wait_recv()
    total = slab[z]
    for d in range(1, depth):
        total = total + slab_in[d - 1]
    final[...] = total

    def gx_copy(d):
        at = ahead(z, d, depth)
        return remote(
            final.at[0:16], first_all.at[y_lo, z], gx_send.at[d], gx_recv.at[y_lo, z],
            device(at, 2 * y_hi + x_lo, x, core),
        )

    def gy_copy(d):
        at = ahead(z, d, depth)
        return remote(
            final.at[16:24], second_all.at[x_lo, z], gy_send.at[d], gy_recv.at[x_lo, z],
            device(at, y, 2 * x_hi + y_lo, core),
        )

    for d in order:
        gx_copy(d).start()
        gy_copy(d).start()

    @pl.when(jnp.logical_not(solver))
    def _():
        gx_copy(0).start()
        gy_copy(0).start()

    def w_copy(k):
        to = plane(*in_plane[k])
        return remote(coef, coefs.at[8 * core + 2 * x + y_hi], w_send.at[k],
                      w_recv.at[8 * core + 2 * x + y_hi], to)

    @pl.when(solver)
    def _():
        pltpu.make_async_copy(final.at[0:16], first_all.at[y_lo, z], gx_recv.at[y_lo, z]).start()
        pltpu.make_async_copy(final.at[16:24], second_all.at[x_lo, z], gy_recv.at[x_lo, z]).start()
        for s in range(2):
            for k in range(8):
                remote(final.at[0:16], first_all.at[s, k], gx_send.at[0], gx_recv.at[s, k],
                       plane(0, 0, 1)).wait_recv()
                remote(final.at[16:24], second_all.at[s, k], gy_send.at[0], gy_recv.at[s, k],
                       plane(0, 0, 1)).wait_recv()
        mixed = first_all[:, :, 0:8, :].reshape(HALF, HALF)
        extra = first_all[0, 0, 8:16, :]
        low = second_all[...].reshape(HALF, HALF)
        coef[...] = solved(mixed, extra, low)
        for k in range(len(in_plane)):
            w_copy(k).start()
        mine = 8 * core + 2 * x + y_hi
        pltpu.make_async_copy(coef, coefs.at[mine], w_recv.at[mine]).start()

    for k in range(LEAVES):
        remote(coef, coefs.at[k], w_send.at[0], w_recv.at[k], plane(0, 0, 1)).wait_recv()
    block = coefs[...]
    weights = jnp.concatenate([block[:, 0, :], block[:, 1, :]], axis=1)
    leaf_output(features, leaf, score, weights, block[:, 2, :], out.at[1], out.at[2])

    def sent(t, carry):
        j = turn(t)
        pair_copy(j).wait_send()

        @pl.when(t < 6)
        def _():
            p1x_copy(t).wait_send()

        @pl.when(row_of(j) != y)
        def _():
            p1y_copy(j).wait_send()

        return carry

    lax.fori_loop(0, 8, sent, 0)
    for d in range(1, 4):
        p2x_copy(d).wait_send()
        p2y_copy(d).wait_send()
    for d in range(1, depth):
        z_copy(d).wait_send()
        gx_copy(d).wait_send()
        gy_copy(d).wait_send()

    @pl.when(jnp.logical_not(solver))
    def _():
        gx_copy(0).wait_send()
        gy_copy(0).wait_send()

    @pl.when(solver)
    def _():
        for k in range(len(in_plane)):
            w_copy(k).wait_send()


def body(features, scores, labels, query_ids, ranks, leaf_ids):
    lines = [x.reshape(BLOCKS, MAXQ) for x in (scores, labels, query_ids, ranks, leaf_ids)]
    dma = pltpu.SemaphoreType.DMA
    tile = lambda *shape: pltpu.VMEM((*shape, HALF), F32)
    out = pl.pallas_call(
        level_kernel,
        out_shape=jax.ShapeDtypeStruct((3, BLOCKS, MAXQ), F32),
        in_specs=[VMEM] * 6,
        out_specs=VMEM,
        scratch_shapes=[
            pltpu.VMEM((F, ROWS), BF16),
            pltpu.VMEM((LEAVES, ROWS), F32),
            tile(6, LEAVES),
            tile(2, 8), tile(8), tile(8),
            tile(8, LEAF_ROWS), tile(8, LEAF_ROWS),
            tile(8, 144), tile(8, 128), tile(3, 2, 144), tile(3, 2, 128),
            tile(4, 72), tile(4, 64), tile(3, 72), tile(3, 64),
            tile(8, 24), tile(7, 24), tile(24), tile(2, 8, 16), tile(2, 8, 8), tile(8),
            tile(LEAVES, 8),
            dma((2,)), dma((2,)), dma((8,)), dma((8,)),
            dma((8,)), dma((3, 2)), dma((8,)), dma((3, 2)),
            dma((3,)), dma((3,)), dma((3,)), dma((3,)),
            dma((7,)), dma((7,)), dma((8,)), dma((2, 8)), dma((8,)), dma((2, 8)),
            dma((31,)), dma((LEAVES,)),
        ],
        compiler_params=pltpu.CompilerParams(collective_id=0, has_side_effects=True),
    )(features, *lines)
    return out[0].reshape(ROWS), out[1].reshape(ROWS), out[2].reshape(ROWS)


def solution(mesh):
    torus = Mesh(mesh.devices.reshape(mesh.shape["doc"] // 2, 2, 4, 2, 2), AXES)
    spec = P(AXES)
    return jax.shard_map(
        body,
        mesh=torus,
        in_specs=(P(AXES, None), spec, spec, spec, spec, spec),
        out_specs=(spec, spec, spec),
        check_vma=False,
    )
```

```python
import jax
import jax.numpy as jnp
from jax import lax
from jax.experimental import pallas as pl
from jax.experimental.pallas import tpu as pltpu
from jax.sharding import Mesh
from jax.sharding import PartitionSpec as P

LEAVES = 16
MAXQ = 128
ROWS = 1024
BLOCKS = ROWS // MAXQ
F = 256
HALF = 128
LEAF_ROWS = 272
AXES = ("z", "y_lo", "x", "y_hi", "core")
MESH = pl.DeviceIdType.MESH
PIVOTS = 8
INNER = slice(MAXQ, ROWS - MAXQ)
DEEP = ROWS - 2 * MAXQ
EDGE = 2 * MAXQ
LAMBDA = 1.0
SHRINKAGE = 0.1
F32 = jnp.float32
BF16 = jnp.bfloat16
NT = (((1,), (1,)), ((), ()))
VMEM = pl.BlockSpec(memory_space=pltpu.VMEM)


def iota(shape, dim):
    return lax.broadcasted_iota(jnp.int32, shape, dim)


def discount(rank_values):
    return 1.0 / jnp.log2(1.0 + jnp.maximum(rank_values, 1.0))


def stacked(rows):
    width = rows[0].shape[1]
    sub = iota((8, width), 0)
    out = jnp.zeros((8, width), F32)
    for k, row in enumerate(rows):
        out = jnp.where(sub == k, jnp.broadcast_to(row, (8, width)), out)
    return out


def pair_sums(own, far_cols, far_ge):
    query, gain, disc, score = own
    far_query, far_gain, far_disc, far_score = far_cols
    same = far_query == query
    gain_gap = gain - far_gain
    score_gap = score - far_score
    signed = jnp.where(same, gain_gap * jnp.abs(disc - far_disc), 0.0)
    prob = 1.0 / (1.0 + jnp.exp(jnp.where(gain_gap >= 0.0, score_gap, -score_gap)))
    pull = signed * prob
    grad = jnp.sum(pull, axis=0, keepdims=True)
    hess = jnp.sum(jnp.abs(pull) * (1.0 - prob), axis=0, keepdims=True)
    mates = jnp.where(same, 1.0, 0.0).astype(BF16)
    counts = jnp.dot(far_ge, mates, preferred_element_type=F32)
    return grad, hess, counts


def far_block(query, label, rank, score):
    gain = jnp.exp2(label)
    disc = discount(rank)
    turned = stacked([query, gain, disc, score]).T
    cols = [jnp.broadcast_to(turned[:, c : c + 1], (MAXQ, MAXQ)) for c in range(4)]
    level = (iota((16, MAXQ), 0) + 1).astype(F32)
    at_least = jnp.where(jnp.broadcast_to(label, (16, MAXQ)) >= level, 1.0, 0.0).astype(BF16)
    return cols, at_least


def own_rows(query_ref, label_ref, rank_ref, score_ref):
    query = query_ref[...].astype(F32)
    label = label_ref[...].astype(F32)
    rank = rank_ref[...].astype(F32)
    return query, label, rank, score_ref[...]


def meet(own, sums, k, far):
    new = pair_sums([x[k : k + 1, :] for x in own], *far)
    sums[k] = new if sums[k] is None else tuple(a + b for a, b in zip(sums[k], new))


def lambdas_within(rows):
    query, label, rank, score = rows
    own = (query, jnp.exp2(label), discount(rank), score)
    sums = [None] * BLOCKS
    for j in range(BLOCKS):
        far = far_block(*[x[j : j + 1, :] for x in rows])
        for k in (j - 1, j, j + 1):
            if 0 <= k < BLOCKS:
                meet(own, sums, k, far)
    return own, sums


def lambdas_across(own, sums, before, after):
    meet(own, sums, 0, far_block(*[before[c : c + 1, :] for c in range(4)]))
    meet(own, sums, BLOCKS - 1, far_block(*[after[c : c + 1, :] for c in range(4)]))


def normalized(sums):
    pull, push, counts = sums
    position = (iota((MAXQ, MAXQ), 0) + 1).astype(F32)
    disc_at = discount(position)
    ideal = jnp.zeros((1, MAXQ), F32)
    for level in range(4):
        inside = jnp.where(position <= counts[level : level + 1, :], disc_at, 0.0)
        ideal = ideal + float(2**level) * jnp.sum(inside, axis=0, keepdims=True)
    inverse = 1.0 / jnp.maximum(ideal, 1.0)
    return -inverse * pull, inverse * push


def leaf_masks(leaf_ref, blocks):
    leaf = leaf_ref[...]
    wide = (LEAVES, MAXQ)
    return [
        jnp.where(jnp.broadcast_to(leaf[k : k + 1, :], wide) == iota(wide, 0), 1.0, 0.0)
        for k in blocks
    ]


def leaf_sums(in_leaf, grads, hess, features, weighted):
    total = lambda parts: jnp.broadcast_to(
        jnp.sum(tree_sum(parts), axis=1, keepdims=True), (LEAVES, MAXQ)
    )
    low = jnp.concatenate([(m * g).astype(BF16) for m, g in zip(in_leaf, grads)], axis=1)
    moment = jnp.dot(low, features, preferred_element_type=F32)
    masks = jnp.concatenate([m.astype(BF16) for m in in_leaf], axis=1)
    hsum = lax.dot_general(masks, weighted, NT, preferred_element_type=F32)
    return [
        hsum[:, :HALF],
        hsum[:, HALF:],
        moment[:, :HALF],
        moment[:, HALF:],
        total([m * h for m, h in zip(in_leaf, hess)]),
        total([m * g for m, g in zip(in_leaf, grads)]),
    ]


def leaf_gram(mask, features, weighted):
    n = features.shape[0]
    own = (weighted.reshape(16, 16, n) * jnp.broadcast_to(mask, (16, n)).astype(BF16)[None])
    gram = jnp.dot(own.reshape(F, n), features, preferred_element_type=F32)
    row = iota((HALF, HALF), 0)
    col = iota((HALF, HALF), 1)
    last = gram[HALF:, HALF:]
    mixed = jnp.where(col <= row, gram[:HALF, :HALF], last)
    diag = jnp.sum(jnp.where(col == row, last, 0.0), axis=0, keepdims=True)
    return mixed, diag, gram[HALF:, :HALF]


def dotted(a, b, dims=(((1,), (0,)), ((), ()))):
    return lax.dot_general(
        a, b, dims, precision=lax.Precision.HIGHEST, preferred_element_type=F32
    )


def tree_sum(terms):
    while len(terms) > 1:
        terms = [sum(terms[k : k + 2][1:], terms[k]) for k in range(0, len(terms), 2)]
    return terms[0]


def small_inverse(d):
    p = len(d)
    if p == 1:
        return [[1.0 / d[0][0]]]
    if p == 2:
        a, b, c = d[0][0], d[0][1], d[1][1]
        r = 1.0 / (a * c - b * b)
        n = -b * r
        return [[c * r, n], [n, a * r]]
    h = p // 2

    def dot(xs, ys):
        return tree_sum([x * y for x, y in zip(xs, ys)])

    first = small_inverse([line[:h] for line in d[:h]])
    side = [line[h:] for line in d[:h]]
    u = [[dot(first[i], [side[m][j] for m in range(h)]) for j in range(h)] for i in range(h)]
    rest = [[None] * h for _ in range(h)]
    for i in range(h):
        for j in range(i, h):
            rest[i][j] = rest[j][i] = d[h + i][h + j] - dot(
                [side[m][i] for m in range(h)], [u[m][j] for m in range(h)]
            )
    last = small_inverse(rest)
    out = [[None] * p for _ in range(p)]
    for i in range(h):
        for j in range(h):
            out[h + i][h + j] = last[i][j]
            out[i][h + j] = out[h + j][i] = -dot(u[i], [last[m][j] for m in range(h)])
    for i in range(h):
        for j in range(i, h):
            out[i][j] = out[j][i] = first[i][j] - dot(
                [out[i][h + m] for m in range(h)], [u[j][m] for m in range(h)]
            )
    return out


def spd_inverse(m, p):
    n = m.shape[0]
    lane = iota((8, n), 1)
    sub = iota((8, n), 0)
    for k in range(0, n, p):
        top = k // 8 * 8
        cols = [jnp.broadcast_to(m[:, k + b : k + b + 1], m.shape) for b in range(p)]
        rows = [jnp.broadcast_to(m[k + a : k + a + 1, :], (8, n)) for a in range(p)]
        d = [[None] * p for _ in range(p)]
        for a in range(p):
            for b in range(a, p):
                d[a][b] = d[b][a] = jnp.broadcast_to(cols[b][k + a : k + a + 1, :], (8, n))
        v = small_inverse(d)
        scaled = []
        for a in range(p):
            r = tree_sum([v[a][b] * rows[b] for b in range(p)])
            for b in range(p):
                r = jnp.where(lane == k + b, v[a][b], r)
            scaled.append(r)
        pivot = (lane >= k) & (lane < k + p)
        tiles = {}
        for t in [(k + p) // 8 * 8 % n] + [t for t in range(0, n, 8) if t != (k + p) // 8 * 8 % n]:
            tile = jnp.where(pivot, 0.0, m[t : t + 8, :])
            tile = tile - tree_sum([cols[a][t : t + 8, :] * scaled[a] for a in range(p)])
            if t == top:
                for a in range(p):
                    tile = jnp.where(sub == k - top + a, scaled[a], tile)
            tiles[t] = tile
        m = jnp.concatenate([tiles[t] for t in range(0, n, 8)], axis=0)
    return m


def solved(mixed, extra, low):
    row = iota((HALF, HALF), 0)
    col = iota((HALF, HALF), 1)
    turned = mixed.T
    hsum = [extra[0:1, :], extra[1:2, :]]
    moment = [extra[2:3, :], extra[3:4, :]]
    htotal, gtotal, diag = extra[4:5, :], extra[5:6, :], extra[6:7, :]
    share = 1.0 / (htotal + LAMBDA)
    scaled = [h * share for h in hsum]
    across = stacked(hsum).T
    over = [jnp.broadcast_to(across[:, k : k + 1], (HALF, HALF)) for k in range(2)]
    unit = jnp.where(row == col, LAMBDA, 0.0)
    a11 = jnp.where(col <= row, mixed, turned) + unit - over[0] * scaled[0]
    a21 = low - over[1] * scaled[0]
    a22 = jnp.where(col > row, mixed, jnp.where(col < row, turned, diag))
    a22 = a22 + unit - over[1] * scaled[1]
    side = [scaled[k] * gtotal - moment[k] for k in range(2)]
    inv1 = spd_inverse(a11, PIVOTS)
    z = dotted(a21, inv1)
    inv2 = spd_inverse(a22 - dotted(z, a21, NT), PIVOTS)
    b1 = jnp.broadcast_to(side[0], (8, HALF))
    b2 = jnp.broadcast_to(side[1], (8, HALF))
    w2 = dotted(b2 - dotted(b1, z, NT), inv2)
    w1 = dotted(b1, inv1) - dotted(w2, z)
    total = jnp.sum(hsum[0] * w1 + hsum[1] * w2, axis=1, keepdims=True)
    c = -(gtotal + total) * share
    return stacked([w1[0:1], w2[0:1], c[0:1]])


def leaf_output(features_ref, leaf_ref, score_ref, weights, intercepts, tree_ref, new_ref):
    high = weights.astype(BF16)
    left = weights - high.astype(F32)
    mid = left.astype(BF16)
    low = (left - mid.astype(F32)).astype(BF16)
    parts = jnp.concatenate([high, mid, low], axis=0)
    sums = lax.dot_general(parts, features_ref[...], NT, preferred_element_type=F32)
    per_leaf = sums[:16] + sums[16:32] + sums[32:48]
    leaf = leaf_ref[...]
    for k in range(BLOCKS):
        rows = slice(MAXQ * k, MAXQ * (k + 1))
        own = jnp.broadcast_to(leaf[k : k + 1, :], (LEAVES, MAXQ)) == iota((LEAVES, MAXQ), 0)
        tree = jnp.sum(
            jnp.where(own, per_leaf[:, rows] + intercepts, 0.0), axis=0, keepdims=True
        )
        tree_ref[k : k + 1, :] = tree
        new_ref[k : k + 1, :] = score_ref[k : k + 1, :] + SHRINKAGE * tree


def position():
    z, y_lo, x, y_hi, core = [lax.axis_index(a) for a in AXES]
    return z, 2 * y_hi + y_lo, x, core


def device(z, y, x, core):
    return (z, lax.rem(y, 2), x, lax.div(y, 2), core)


def neighbour(by):
    index = jnp.int32(0)
    total = 1
    for a in AXES:
        index = index * lax.axis_size(a) + lax.axis_index(a)
        total *= lax.axis_size(a)
    index = lax.rem(index + by + total, total)
    place = []
    for a in reversed(AXES):
        place.append(lax.rem(index, lax.axis_size(a)))
        index = lax.div(index, lax.axis_size(a))
    return tuple(reversed(place))


def ahead(value, by, size):
    return lax.rem(value + by, size)


def level_kernel(
    features, score, label, query, rank, leaf,
    out,
    inner_weighted, edge_turned, edge_weighted, edge_features, in_leaf, sums_ref,
    inner_mixed, inner_diag, inner_low,
    edge, before, after,
    pair_out, pair_in,
    first_sum, second_sum, first_in, second_in,
    first_part, second_part, first_in2, second_in2,
    slab, slab_in, final, first_all, second_all, coef, coefs,
    halo_send, halo_recv, pair_send, pair_recv,
    p1x_send, p1x_recv, p1y_send, p1y_recv,
    p2x_send, p2x_recv, p2y_send, p2y_recv,
    z_send, z_recv, gx_send, gx_recv, gy_send, gy_recv,
    w_send, w_recv,
):
    z, y, x, core = position()
    depth = lax.axis_size("z")
    y_lo, x_lo = lax.rem(y, 2), lax.rem(x, 2)
    y_hi, x_hi = lax.div(y, 2), lax.div(x, 2)
    y_pair, x_pair = y + 1 - 2 * y_lo, x + 1 - 2 * x_lo
    other = 1 - core
    solver = x_lo == y_lo
    in_plane = [
        (dx, dy, dc) for dx in (2, 1, 3, 0) for dy in (2, 1, 3, 0) for dc in (1, 0) if dx or dy or dc
    ]

    def plane(dx, dy, dc):
        return device(z, ahead(y, dy, 4), ahead(x, dx, 4), ahead(core, dc, 2))

    barrier = pltpu.get_barrier_semaphore()
    partners = [neighbour(1), neighbour(-1)] + [plane(*d) for d in in_plane]
    for d in range(1, depth):
        at = ahead(z, d, depth)
        partners += [device(at, y, x, core), device(at, y_pair, x, core), device(at, y, x_pair, core)]
    for partner in partners:
        pl.semaphore_signal(barrier, inc=1, device_id=partner, device_id_type=MESH)

    def remote(src, dst, send, recv, to):
        return pltpu.make_async_remote_copy(
            src_ref=src, dst_ref=dst, send_sem=send, recv_sem=recv, device_id=to, device_id_type=MESH
        )

    rows = own_rows(query, label, rank, score)
    edge[0] = stacked([r[BLOCKS - 1 : BLOCKS, :] for r in rows])
    edge[1] = stacked([r[0:1, :] for r in rows])
    own, sums = lambdas_within(rows)

    inner = range(1, BLOCKS - 1)
    ends = (0, BLOCKS - 1)
    grads, hess = {}, {}
    for b in range(BLOCKS):
        turned = features[MAXQ * b : MAXQ * (b + 1), :].astype(F32).T
        if b in inner:
            grads[b], hess[b] = normalized(sums[b])
            out[0, b : b + 1, :] = grads[b]
            inner_weighted[:, MAXQ * (b - 1) : MAXQ * b] = (turned * hess[b]).astype(BF16)
        else:
            place = MAXQ * ends.index(b)
            edge_turned[:, place : place + MAXQ] = turned.astype(BF16)
            edge_features[place : place + MAXQ, :] = features[MAXQ * b : MAXQ * (b + 1), :]
    masks = leaf_masks(leaf, inner)
    for b in inner:
        in_leaf[:, MAXQ * (b - 1) : MAXQ * b] = masks[b - 1]
    end_masks = leaf_masks(leaf, ends)
    in_leaf[:, DEEP : DEEP + MAXQ] = end_masks[0]
    in_leaf[:, DEEP + MAXQ :] = end_masks[1]
    small = leaf_sums(
        masks, [grads[b] for b in inner], [hess[b] for b in inner], features[INNER, :], inner_weighted[...]
    )
    for k in range(6):
        sums_ref[k] = small[k]

    def inner_leaf(number, carry):
        mixed, diag, low = leaf_gram(
            in_leaf[pl.ds(number, 1), :DEEP], features[INNER, :], inner_weighted[...]
        )
        inner_mixed[number] = mixed
        inner_diag[number] = jnp.broadcast_to(diag, (8, HALF))
        inner_low[number] = low
        return carry

    lax.fori_loop(0, LEAVES, inner_leaf, 0)
    pl.semaphore_wait(barrier, len(partners))

    later, earlier = neighbour(1), neighbour(-1)
    to_later = remote(edge.at[0], before, halo_send.at[0], halo_recv.at[0], later)
    to_earlier = remote(edge.at[1], after, halo_send.at[1], halo_recv.at[1], earlier)
    to_later.start()
    to_earlier.start()
    to_later.wait()
    to_earlier.wait()
    first_device = (z == 0) & (y_lo == 0) & (x == 0) & (y_hi == 0) & (core == 0)
    last_device = (z == depth - 1) & (y_lo == 1) & (x == 3) & (y_hi == 1) & (core == 1)
    top = iota((8, MAXQ), 0) == 0
    was = jnp.where(top & first_device, -1.0, before[...])
    will = jnp.where(top & last_device, -1.0, after[...])
    lambdas_across(own, sums, was, will)
    for b in ends:
        grads[b], hess[b] = normalized(sums[b])
        out[0, b : b + 1, :] = grads[b]
        place = MAXQ * ends.index(b)
        turned = edge_turned[:, place : place + MAXQ].astype(F32)
        edge_weighted[:, place : place + MAXQ] = (turned * hess[b]).astype(BF16)
    small = leaf_sums(
        end_masks, [grads[b] for b in ends], [hess[b] for b in ends], edge_features[...], edge_weighted[...]
    )
    for k in range(6):
        sums_ref[k] = sums_ref[k] + small[k]

    def packed_leaf(number):
        mixed, diag, low = leaf_gram(
            in_leaf[pl.ds(number, 1), DEEP:], edge_features[...], edge_weighted[...]
        )
        mixed = mixed + inner_mixed[number]
        extra = [sums_ref[k, pl.ds(number, 1), :] for k in range(6)]
        extra = stacked(extra + [diag + inner_diag[number, 0:1, :]])
        first = jnp.concatenate(
            [mixed[:64], extra, mixed[64:], jnp.zeros((8, HALF), F32)], axis=0
        )
        return first, low + inner_low[number]

    def turn(t):
        return lax.rem(2 * (x + 1) + t, 8)

    def pair_copy(j):
        return remote(
            pair_out.at[j], pair_in.at[j], pair_send.at[j], pair_recv.at[j], plane(0, 0, 1)
        )

    def for_other(t, carry):
        j = turn(t)
        number = 8 * other + j
        first, second = packed_leaf(number)
        pair_out[j, :144, :] = first
        pair_out[j, 144:, :] = second
        pair_copy(j).start()
        return carry

    lax.fori_loop(0, 8, for_other, 0)

    def p1x_copy(t):
        j, d = turn(t), lax.div(t, 2) + 1
        return remote(
            first_sum.at[j],
            first_in.at[d - 1, lax.rem(t, 2)],
            p1x_send.at[j],
            p1x_recv.at[d - 1, lax.rem(t, 2)],
            device(z, y, ahead(x, d, 4), core),
        )

    def row_of(j):
        return 2 * lax.rem(j, 2) + lax.rem(lax.div(j, 2), 2)

    def p1y_copy(j):
        d = lax.rem(row_of(j) - y + 4, 4)
        return remote(
            second_sum.at[j],
            second_in.at[lax.rem(d + 3, 4), lax.div(j, 4)],
            p1y_send.at[j],
            p1y_recv.at[lax.rem(d + 3, 4), lax.div(j, 4)],
            device(z, row_of(j), x, core),
        )

    def for_own(t, carry):
        j = turn(t)
        number = 8 * core + j
        first, second = packed_leaf(number)
        pair_copy(j).wait_recv()
        first_sum[j] = first + pair_in[j, :144, :]
        second_sum[j] = second + pair_in[j, 144:, :]

        @pl.when(t < 6)
        def _():
            p1x_copy(t).start()

        @pl.when(row_of(j) != y)
        def _():
            p1y_copy(j).start()

        return carry

    lax.fori_loop(0, 8, for_own, 0)

    for h in range(2):
        for d in range(1, 4):
            p1x_copy(2 * (d - 1) + h).wait_recv()
        total = first_sum[2 * x + h] + first_in[0, h] + first_in[1, h] + first_in[2, h]
        first_part[2 * h] = total[:72]
        first_part[2 * h + 1] = total[72:]

    def p2x_copy(d):
        at = ahead(y, d, 4)
        return remote(
            first_part.at[at], first_in2.at[d - 1], p2x_send.at[d - 1], p2x_recv.at[d - 1],
            device(z, at, x, core),
        )

    def p2y_copy(d):
        at = ahead(x, d, 4)
        return remote(
            second_part.at[at], second_in2.at[d - 1], p2y_send.at[d - 1], p2y_recv.at[d - 1],
            device(z, y, at, core),
        )

    for d in (2, 1, 3):
        p2x_copy(d).start()
    for u in range(2):
        for d in range(1, 4):
            remote(
                second_sum.at[0], second_in.at[d - 1, u], p1y_send.at[0], p1y_recv.at[d - 1, u],
                device(z, ahead(y, d, 4), x, core),
            ).wait_recv()
        j = 4 * u + 2 * y_lo + y_hi
        total = second_sum[j] + second_in[0, u] + second_in[1, u] + second_in[2, u]
        second_part[2 * u] = total[:64]
        second_part[2 * u + 1] = total[64:]
    for d in (2, 1, 3):
        p2y_copy(d).start()

    for d in range(1, 4):
        p2x_copy(d).wait_recv()
    total = first_part[y] + first_in2[0] + first_in2[1] + first_in2[2]
    slab[:, 0:8, :] = total[:64].reshape(8, 8, HALF)
    slab[:, 8:16, :] = jnp.broadcast_to(total[64:][None], (8, 8, HALF))
    for d in range(1, 4):
        p2y_copy(d).wait_recv()
    total = second_part[x] + second_in2[0] + second_in2[1] + second_in2[2]
    slab[:, 16:24, :] = total.reshape(8, 8, HALF)

    def z_copy(d):
        at = ahead(z, d, depth)
        return remote(
            slab.at[at], slab_in.at[d - 1], z_send.at[d - 1], z_recv.at[d - 1],
            device(at, y, x, core),
        )

    order = (4, 3, 5, 2, 6, 1, 7)
    for d in order:
        z_copy(d).start()
    for d in order:
        z_copy(d).wait_recv()
    total = slab[z]
    for d in range(1, depth):
        total = total + slab_in[d - 1]
    final[...] = total

    def gx_copy(d):
        at = ahead(z, d, depth)
        return remote(
            final.at[0:16], first_all.at[y_lo, z], gx_send.at[d], gx_recv.at[y_lo, z],
            device(at, 2 * y_hi + x_lo, x, core),
        )

    def gy_copy(d):
        at = ahead(z, d, depth)
        return remote(
            final.at[16:24], second_all.at[x_lo, z], gy_send.at[d], gy_recv.at[x_lo, z],
            device(at, y, 2 * x_hi + y_lo, core),
        )

    for d in order:
        gx_copy(d).start()
        gy_copy(d).start()

    @pl.when(jnp.logical_not(solver))
    def _():
        gx_copy(0).start()
        gy_copy(0).start()

    def w_copy(k):
        to = plane(*in_plane[k])
        return remote(coef, coefs.at[8 * core + 2 * x + y_hi], w_send.at[k],
                      w_recv.at[8 * core + 2 * x + y_hi], to)

    @pl.when(solver)
    def _():
        pltpu.make_async_copy(final.at[0:16], first_all.at[y_lo, z], gx_recv.at[y_lo, z]).start()
        pltpu.make_async_copy(final.at[16:24], second_all.at[x_lo, z], gy_recv.at[x_lo, z]).start()
        for s in range(2):
            for k in range(8):
                remote(final.at[0:16], first_all.at[s, k], gx_send.at[0], gx_recv.at[s, k],
                       plane(0, 0, 1)).wait_recv()
                remote(final.at[16:24], second_all.at[s, k], gy_send.at[0], gy_recv.at[s, k],
                       plane(0, 0, 1)).wait_recv()
        mixed = first_all[:, :, 0:8, :].reshape(HALF, HALF)
        extra = first_all[0, 0, 8:16, :]
        low = second_all[...].reshape(HALF, HALF)
        coef[...] = solved(mixed, extra, low)
        for k in range(len(in_plane)):
            w_copy(k).start()
        mine = 8 * core + 2 * x + y_hi
        pltpu.make_async_copy(coef, coefs.at[mine], w_recv.at[mine]).start()

    for k in range(LEAVES):
        remote(coef, coefs.at[k], w_send.at[0], w_recv.at[k], plane(0, 0, 1)).wait_recv()
    block = coefs[...]
    weights = jnp.concatenate([block[:, 0, :], block[:, 1, :]], axis=1)
    leaf_output(features, leaf, score, weights, block[:, 2, :], out.at[1], out.at[2])

    def sent(t, carry):
        j = turn(t)
        pair_copy(j).wait_send()

        @pl.when(t < 6)
        def _():
            p1x_copy(t).wait_send()

        @pl.when(row_of(j) != y)
        def _():
            p1y_copy(j).wait_send()

        return carry

    lax.fori_loop(0, 8, sent, 0)
    for d in range(1, 4):
        p2x_copy(d).wait_send()
        p2y_copy(d).wait_send()
    for d in range(1, depth):
        z_copy(d).wait_send()
        gx_copy(d).wait_send()
        gy_copy(d).wait_send()

    @pl.when(jnp.logical_not(solver))
    def _():
        gx_copy(0).wait_send()
        gy_copy(0).wait_send()

    @pl.when(solver)
    def _():
        for k in range(len(in_plane)):
            w_copy(k).wait_send()


def body(features, scores, labels, query_ids, ranks, leaf_ids):
    lines = [x.reshape(BLOCKS, MAXQ) for x in (scores, labels, query_ids, ranks, leaf_ids)]
    dma = pltpu.SemaphoreType.DMA
    tile = lambda *shape: pltpu.VMEM((*shape, HALF), F32)
    out = pl.pallas_call(
        level_kernel,
        out_shape=jax.ShapeDtypeStruct((3, BLOCKS, MAXQ), F32),
        in_specs=[VMEM] * 6,
        out_specs=VMEM,
        scratch_shapes=[
            pltpu.VMEM((F, DEEP), BF16),
            pltpu.VMEM((F, EDGE), BF16),
            pltpu.VMEM((F, EDGE), BF16),
            pltpu.VMEM((EDGE, F), BF16),
            pltpu.VMEM((LEAVES, ROWS), F32),
            tile(6, LEAVES),
            tile(LEAVES, HALF), tile(LEAVES, 8), tile(LEAVES, HALF),
            tile(2, 8), tile(8), tile(8),
            tile(8, LEAF_ROWS), tile(8, LEAF_ROWS),
            tile(8, 144), tile(8, 128), tile(3, 2, 144), tile(3, 2, 128),
            tile(4, 72), tile(4, 64), tile(3, 72), tile(3, 64),
            tile(8, 24), tile(7, 24), tile(24), tile(2, 8, 16), tile(2, 8, 8), tile(8),
            tile(LEAVES, 8),
            dma((2,)), dma((2,)), dma((8,)), dma((8,)),
            dma((8,)), dma((3, 2)), dma((8,)), dma((3, 2)),
            dma((3,)), dma((3,)), dma((3,)), dma((3,)),
            dma((7,)), dma((7,)), dma((8,)), dma((2, 8)), dma((8,)), dma((2, 8)),
            dma((31,)), dma((LEAVES,)),
        ],
        compiler_params=pltpu.CompilerParams(collective_id=0, has_side_effects=True),
    )(features, *lines)
    return out[0].reshape(ROWS), out[1].reshape(ROWS), out[2].reshape(ROWS)


def solution(mesh):
    torus = Mesh(mesh.devices.reshape(mesh.shape["doc"] // 2, 2, 4, 2, 2), AXES)
    spec = P(AXES)
    return jax.shard_map(
        body,
        mesh=torus,
        in_specs=(P(AXES, None), spec, spec, spec, spec, spec),
        out_specs=(spec, spec, spec),
        check_vma=False,
    )
```

```python
import jax
import jax.numpy as jnp
from jax import lax
from jax.experimental import pallas as pl
from jax.experimental.pallas import tpu as pltpu
from jax.sharding import Mesh
from jax.sharding import PartitionSpec as P

LEAVES = 16
MAXQ = 128
ROWS = 1024
BLOCKS = ROWS // MAXQ
F = 256
HALF = 128
LEAF_ROWS = 272
AXES = ("z", "y_lo", "x", "y_hi", "core")
MESH = pl.DeviceIdType.MESH
PIVOTS = 8
INNER = slice(MAXQ, ROWS - MAXQ)
DEEP = ROWS - 2 * MAXQ
EDGE = 2 * MAXQ
LAMBDA = 1.0
SHRINKAGE = 0.1
F32 = jnp.float32
BF16 = jnp.bfloat16
NT = (((1,), (1,)), ((), ()))
VMEM = pl.BlockSpec(memory_space=pltpu.VMEM)


def iota(shape, dim):
    return lax.broadcasted_iota(jnp.int32, shape, dim)


def discount(rank_values):
    return 1.0 / jnp.log2(1.0 + jnp.maximum(rank_values, 1.0))


def stacked(rows):
    width = rows[0].shape[1]
    sub = iota((8, width), 0)
    out = jnp.zeros((8, width), F32)
    for k, row in enumerate(rows):
        out = jnp.where(sub == k, jnp.broadcast_to(row, (8, width)), out)
    return out


def pair_sums(own, far_cols, far_ge):
    query, gain, disc, score = own
    far_query, far_gain, far_disc, far_score = far_cols
    same = far_query == query
    gain_gap = gain - far_gain
    score_gap = score - far_score
    signed = jnp.where(same, gain_gap * jnp.abs(disc - far_disc), 0.0)
    prob = 1.0 / (1.0 + jnp.exp(jnp.where(gain_gap >= 0.0, score_gap, -score_gap)))
    pull = signed * prob
    grad = jnp.sum(pull, axis=0, keepdims=True)
    hess = jnp.sum(jnp.abs(pull) * (1.0 - prob), axis=0, keepdims=True)
    mates = jnp.where(same, 1.0, 0.0).astype(BF16)
    counts = jnp.dot(far_ge, mates, preferred_element_type=F32)
    return grad, hess, counts


def far_block(query, label, rank, score):
    gain = jnp.exp2(label)
    disc = discount(rank)
    turned = stacked([query, gain, disc, score]).T
    cols = [jnp.broadcast_to(turned[:, c : c + 1], (MAXQ, MAXQ)) for c in range(4)]
    level = (iota((16, MAXQ), 0) + 1).astype(F32)
    at_least = jnp.where(jnp.broadcast_to(label, (16, MAXQ)) >= level, 1.0, 0.0).astype(BF16)
    return cols, at_least


def own_rows(query_ref, label_ref, rank_ref, score_ref):
    query = query_ref[...].astype(F32)
    label = label_ref[...].astype(F32)
    rank = rank_ref[...].astype(F32)
    return query, label, rank, score_ref[...]


def meet(own, sums, k, far):
    new = pair_sums([x[k : k + 1, :] for x in own], *far)
    sums[k] = new if sums[k] is None else tuple(a + b for a, b in zip(sums[k], new))


def lambdas_within(rows):
    query, label, rank, score = rows
    own = (query, jnp.exp2(label), discount(rank), score)
    sums = [None] * BLOCKS
    for j in range(BLOCKS):
        far = far_block(*[x[j : j + 1, :] for x in rows])
        for k in (j - 1, j, j + 1):
            if 0 <= k < BLOCKS:
                meet(own, sums, k, far)
    return own, sums


def added(first, second):
    return tuple(a + b for a, b in zip(first, second))


def normalized(sums):
    pull, push, counts = sums
    position = (iota((MAXQ, MAXQ), 0) + 1).astype(F32)
    disc_at = discount(position)
    ideal = jnp.zeros((1, MAXQ), F32)
    for level in range(4):
        inside = jnp.where(position <= counts[level : level + 1, :], disc_at, 0.0)
        ideal = ideal + float(2**level) * jnp.sum(inside, axis=0, keepdims=True)
    inverse = 1.0 / jnp.maximum(ideal, 1.0)
    return -inverse * pull, inverse * push


def leaf_mask(leaf):
    wide = (LEAVES, MAXQ)
    return jnp.where(jnp.broadcast_to(leaf, wide) == iota(wide, 0).astype(F32), 1.0, 0.0)


def leaf_sums(in_leaf, grads, hess, features, weighted):
    total = lambda parts: jnp.broadcast_to(
        jnp.sum(tree_sum(parts), axis=1, keepdims=True), (LEAVES, MAXQ)
    )
    low = jnp.concatenate([(m * g).astype(BF16) for m, g in zip(in_leaf, grads)], axis=1)
    moment = jnp.dot(low, features, preferred_element_type=F32)
    masks = jnp.concatenate([m.astype(BF16) for m in in_leaf], axis=1)
    hsum = lax.dot_general(masks, weighted, NT, preferred_element_type=F32)
    return [
        hsum[:, :HALF],
        hsum[:, HALF:],
        moment[:, :HALF],
        moment[:, HALF:],
        total([m * h for m, h in zip(in_leaf, hess)]),
        total([m * g for m, g in zip(in_leaf, grads)]),
    ]


def leaf_gram(mask, features, weighted):
    n = features.shape[0]
    own = (weighted.reshape(16, 16, n) * jnp.broadcast_to(mask, (16, n)).astype(BF16)[None])
    gram = jnp.dot(own.reshape(F, n), features, preferred_element_type=F32)
    row = iota((HALF, HALF), 0)
    col = iota((HALF, HALF), 1)
    last = gram[HALF:, HALF:]
    mixed = jnp.where(col <= row, gram[:HALF, :HALF], last)
    diag = jnp.sum(jnp.where(col == row, last, 0.0), axis=0, keepdims=True)
    return mixed, diag, gram[HALF:, :HALF]


def dotted(a, b, dims=(((1,), (0,)), ((), ()))):
    return lax.dot_general(
        a, b, dims, precision=lax.Precision.HIGHEST, preferred_element_type=F32
    )


def tree_sum(terms):
    while len(terms) > 1:
        terms = [sum(terms[k : k + 2][1:], terms[k]) for k in range(0, len(terms), 2)]
    return terms[0]


def small_inverse(d):
    p = len(d)
    if p == 1:
        return [[1.0 / d[0][0]]]
    if p == 2:
        a, b, c = d[0][0], d[0][1], d[1][1]
        r = 1.0 / (a * c - b * b)
        n = -b * r
        return [[c * r, n], [n, a * r]]
    h = p // 2

    def dot(xs, ys):
        return tree_sum([x * y for x, y in zip(xs, ys)])

    first = small_inverse([line[:h] for line in d[:h]])
    side = [line[h:] for line in d[:h]]
    u = [[dot(first[i], [side[m][j] for m in range(h)]) for j in range(h)] for i in range(h)]
    rest = [[None] * h for _ in range(h)]
    for i in range(h):
        for j in range(i, h):
            rest[i][j] = rest[j][i] = d[h + i][h + j] - dot(
                [side[m][i] for m in range(h)], [u[m][j] for m in range(h)]
            )
    last = small_inverse(rest)
    out = [[None] * p for _ in range(p)]
    for i in range(h):
        for j in range(h):
            out[h + i][h + j] = last[i][j]
            out[i][h + j] = out[h + j][i] = -dot(u[i], [last[m][j] for m in range(h)])
    for i in range(h):
        for j in range(i, h):
            out[i][j] = out[j][i] = first[i][j] - dot(
                [out[i][h + m] for m in range(h)], [u[j][m] for m in range(h)]
            )
    return out


def spd_inverse(m, p):
    n = m.shape[0]
    lane = iota((8, n), 1)
    sub = iota((8, n), 0)
    for k in range(0, n, p):
        top = k // 8 * 8
        cols = [jnp.broadcast_to(m[:, k + b : k + b + 1], m.shape) for b in range(p)]
        rows = [jnp.broadcast_to(m[k + a : k + a + 1, :], (8, n)) for a in range(p)]
        d = [[None] * p for _ in range(p)]
        for a in range(p):
            for b in range(a, p):
                d[a][b] = d[b][a] = jnp.broadcast_to(cols[b][k + a : k + a + 1, :], (8, n))
        v = small_inverse(d)
        scaled = []
        for a in range(p):
            r = tree_sum([v[a][b] * rows[b] for b in range(p)])
            for b in range(p):
                r = jnp.where(lane == k + b, v[a][b], r)
            scaled.append(r)
        pivot = (lane >= k) & (lane < k + p)
        tiles = {}
        for t in [(k + p) // 8 * 8 % n] + [t for t in range(0, n, 8) if t != (k + p) // 8 * 8 % n]:
            tile = jnp.where(pivot, 0.0, m[t : t + 8, :])
            tile = tile - tree_sum([cols[a][t : t + 8, :] * scaled[a] for a in range(p)])
            if t == top:
                for a in range(p):
                    tile = jnp.where(sub == k - top + a, scaled[a], tile)
            tiles[t] = tile
        m = jnp.concatenate([tiles[t] for t in range(0, n, 8)], axis=0)
    return m


def solved(mixed, extra, low):
    row = iota((HALF, HALF), 0)
    col = iota((HALF, HALF), 1)
    turned = mixed.T
    hsum = [extra[0:1, :], extra[1:2, :]]
    moment = [extra[2:3, :], extra[3:4, :]]
    htotal, gtotal, diag = extra[4:5, :], extra[5:6, :], extra[6:7, :]
    share = 1.0 / (htotal + LAMBDA)
    scaled = [h * share for h in hsum]
    across = stacked(hsum).T
    over = [jnp.broadcast_to(across[:, k : k + 1], (HALF, HALF)) for k in range(2)]
    unit = jnp.where(row == col, LAMBDA, 0.0)
    a11 = jnp.where(col <= row, mixed, turned) + unit - over[0] * scaled[0]
    a21 = low - over[1] * scaled[0]
    a22 = jnp.where(col > row, mixed, jnp.where(col < row, turned, diag))
    a22 = a22 + unit - over[1] * scaled[1]
    side = [scaled[k] * gtotal - moment[k] for k in range(2)]
    inv1 = spd_inverse(a11, PIVOTS)
    z = dotted(a21, inv1)
    inv2 = spd_inverse(a22 - dotted(z, a21, NT), PIVOTS)
    b1 = jnp.broadcast_to(side[0], (8, HALF))
    b2 = jnp.broadcast_to(side[1], (8, HALF))
    w2 = dotted(b2 - dotted(b1, z, NT), inv2)
    w1 = dotted(b1, inv1) - dotted(w2, z)
    total = jnp.sum(hsum[0] * w1 + hsum[1] * w2, axis=1, keepdims=True)
    c = -(gtotal + total) * share
    return stacked([w1[0:1], w2[0:1], c[0:1]])


def leaf_output(features_ref, leaf_ref, score_ref, weights, intercepts, tree_ref, new_ref):
    high = weights.astype(BF16)
    left = weights - high.astype(F32)
    mid = left.astype(BF16)
    low = (left - mid.astype(F32)).astype(BF16)
    parts = jnp.concatenate([high, mid, low], axis=0)
    sums = lax.dot_general(parts, features_ref[...], NT, preferred_element_type=F32)
    per_leaf = sums[:16] + sums[16:32] + sums[32:48]
    leaf = leaf_ref[...]
    for k in range(BLOCKS):
        rows = slice(MAXQ * k, MAXQ * (k + 1))
        own = jnp.broadcast_to(leaf[k : k + 1, :], (LEAVES, MAXQ)) == iota((LEAVES, MAXQ), 0)
        tree = jnp.sum(
            jnp.where(own, per_leaf[:, rows] + intercepts, 0.0), axis=0, keepdims=True
        )
        tree_ref[k : k + 1, :] = tree
        new_ref[k : k + 1, :] = score_ref[k : k + 1, :] + SHRINKAGE * tree


def position():
    z, y_lo, x, y_hi, core = [lax.axis_index(a) for a in AXES]
    return z, 2 * y_hi + y_lo, x, core


def device(z, y, x, core):
    return (z, lax.rem(y, 2), x, lax.div(y, 2), core)


def neighbour(by):
    index = jnp.int32(0)
    total = 1
    for a in AXES:
        index = index * lax.axis_size(a) + lax.axis_index(a)
        total *= lax.axis_size(a)
    index = lax.rem(index + by + total, total)
    place = []
    for a in reversed(AXES):
        place.append(lax.rem(index, lax.axis_size(a)))
        index = lax.div(index, lax.axis_size(a))
    return tuple(reversed(place))


def ahead(value, by, size):
    return lax.rem(value + by, size)


def level_kernel(
    features, score, label, query, rank, leaf,
    out,
    inner_weighted, outer_turned, outer_weighted, outer_features, in_leaf, sums_ref, end_sums,
    inner_mixed, inner_diag, inner_low,
    edge, halo, info, info_in, outer_out, outer_in,
    pair_out, pair_in,
    first_sum, second_sum, first_in, second_in,
    first_part, second_part, first_in2, second_in2,
    slab, slab_in, final, first_all, second_all, coef, coefs,
    halo_send, halo_recv, mate_send, mate_recv, pair_send, pair_recv,
    p1x_send, p1x_recv, p1y_send, p1y_recv,
    p2x_send, p2x_recv, p2y_send, p2y_recv,
    z_send, z_recv, gx_send, gx_recv, gy_send, gy_recv,
    w_send, w_recv,
):
    z, y, x, core = position()
    depth = lax.axis_size("z")
    y_lo, x_lo = lax.rem(y, 2), lax.rem(x, 2)
    y_hi, x_hi = lax.div(y, 2), lax.div(x, 2)
    y_pair, x_pair = y + 1 - 2 * y_lo, x + 1 - 2 * x_lo
    other = 1 - core
    solver = x_lo == y_lo
    in_plane = [
        (dx, dy, dc) for dx in (2, 1, 3, 0) for dy in (2, 1, 3, 0) for dc in (1, 0) if dx or dy or dc
    ]

    def plane(dx, dy, dc):
        return device(z, ahead(y, dy, 4), ahead(x, dx, 4), ahead(core, dc, 2))

    def pick(a, b):
        return jnp.where(core == 0, a, b)

    barrier = pltpu.get_barrier_semaphore()
    partners = [neighbour(by - core) for by in (-2, -1, 2, 3)] + [plane(*d) for d in in_plane]
    for d in range(1, depth):
        at = ahead(z, d, depth)
        partners += [device(at, y, x, core), device(at, y_pair, x, core), device(at, y, x_pair, core)]
    for partner in partners:
        pl.semaphore_signal(barrier, inc=1, device_id=partner, device_id_type=MESH)

    def remote(src, dst, send, recv, to):
        return pltpu.make_async_remote_copy(
            src_ref=src, dst_ref=dst, send_sem=send, recv_sem=recv, device_id=to, device_id_type=MESH
        )

    rows = own_rows(query, label, rank, score)
    leaves = leaf[...].astype(F32)
    edge[0] = stacked([r[BLOCKS - 1 : BLOCKS, :] for r in rows])
    edge[1] = stacked([r[0:1, :] for r in rows])
    for k in range(4):
        info[k] = rows[k]
    info[4] = leaves
    outer_start = pl.multiple_of(core * (ROWS - MAXQ), MAXQ)
    middle_start = pl.multiple_of(other * (ROWS - MAXQ), MAXQ)
    outer_out[...] = features[pl.ds(outer_start, MAXQ), :].astype(F32)
    own, sums = lambdas_within(rows)

    inner = range(1, BLOCKS - 1)
    grads, hess = [], []
    for b in inner:
        turned = features[MAXQ * b : MAXQ * (b + 1), :].astype(F32).T
        g, h = normalized(sums[b])
        grads.append(g)
        hess.append(h)
        out[0, b : b + 1, :] = g
        inner_weighted[:, MAXQ * (b - 1) : MAXQ * b] = (turned * h).astype(BF16)
    masks = [leaf_mask(leaves[b : b + 1, :]) for b in inner]
    for b in inner:
        in_leaf[:, MAXQ * (b - 1) : MAXQ * b] = masks[b - 1]
    small = leaf_sums(masks, grads, hess, features[INNER, :], inner_weighted[...])
    for k in range(6):
        sums_ref[k] = small[k]
    middle_turned = outer_weighted.at[:, :MAXQ]
    middle_turned[...] = features[pl.ds(middle_start, MAXQ), :].astype(F32).T.astype(BF16)
    outer_turned[:, :MAXQ] = outer_out[...].T.astype(BF16)
    outer_features[:MAXQ, :] = features[pl.ds(outer_start, MAXQ), :]

    def inner_leaf(number, carry):
        mixed, diag, low = leaf_gram(
            in_leaf[pl.ds(number, 1), :DEEP], features[INNER, :], inner_weighted[...]
        )
        inner_mixed[number] = mixed
        inner_diag[number] = jnp.broadcast_to(diag, (8, HALF))
        inner_low[number] = low
        return carry

    lax.fori_loop(0, LEAVES, inner_leaf, 0)
    pl.semaphore_wait(barrier, len(partners))

    halos = [
        remote(
            edge.at[other], halo.at[other], halo_send.at[k], halo_recv.at[other],
            neighbour(pick(-2, 1) + k),
        )
        for k in range(2)
    ]
    for copy in halos:
        copy.start()
    info_copy = remote(info, info_in, mate_send.at[0], mate_recv.at[0], plane(0, 0, 1))
    outer_copy = remote(outer_out, outer_in, mate_send.at[1], mate_recv.at[1], plane(0, 0, 1))
    info_copy.start()
    outer_copy.start()
    info_copy.wait_recv()

    mate = [info_in[k] for k in range(4)]
    beside = far_block(*[pick(r[:1], r[BLOCKS - 1 :]) for r in mate])
    middle = [pick(r[BLOCKS - 1 :], r[:1]) for r in own]
    middle_sums = tuple(pick(a, b) for a, b in zip(sums[BLOCKS - 1], sums[0]))
    g, h = normalized(added(middle_sums, pair_sums(middle, *beside)))
    out[0, pl.ds(other * (BLOCKS - 1), 1), :] = g
    middle_weighted = (middle_turned[...].astype(F32) * h).astype(BF16)
    middle_mask = leaf_mask(pick(leaves[BLOCKS - 1 :], leaves[:1]))
    middle_features = features[pl.ds(middle_start, MAXQ), :]
    in_leaf[:, DEEP : DEEP + MAXQ] = middle_mask
    small = leaf_sums([middle_mask], [g], [h], middle_features, middle_weighted)
    for k in range(6):
        sums_ref[k] = sums_ref[k] + small[k]
    outer_weighted[:, :MAXQ] = middle_weighted

    def chip_leaf(number):
        mixed, diag, low = leaf_gram(
            in_leaf[pl.ds(number, 1), DEEP : DEEP + 2 * MAXQ][:, :MAXQ],
            features[pl.ds(middle_start, MAXQ), :],
            outer_weighted[:, :MAXQ],
        )
        mixed = mixed + inner_mixed[number]
        extra = [sums_ref[k, pl.ds(number, 1), :] for k in range(6)]
        extra = stacked(extra + [diag + inner_diag[number, 0:1, :]])
        first = jnp.concatenate(
            [mixed[:64], extra, mixed[64:], jnp.zeros((8, HALF), F32)], axis=0
        )
        return first, low + inner_low[number]

    def turn(t):
        return lax.rem(2 * (x + 1) + t, 8)

    def pair_copy(j):
        return remote(
            pair_out.at[j], pair_in.at[j], pair_send.at[j], pair_recv.at[j], plane(0, 0, 1)
        )

    def for_other(t, carry):
        j = turn(t)
        first, second = chip_leaf(8 * other + j)
        pair_out[j, :144, :] = first
        pair_out[j, 144:, :] = second
        pair_copy(j).start()
        return carry

    lax.fori_loop(0, 8, for_other, 0)

    def for_own_rows(t, carry):
        j = turn(t)
        first, second = chip_leaf(8 * core + j)
        first_sum[j] = first
        second_sum[j] = second
        return carry

    lax.fori_loop(0, 8, for_own_rows, 0)
    mate_outer = [pick(r[BLOCKS - 1 :], r[:1]) for r in mate]
    mate_next = [pick(r[BLOCKS - 2 : BLOCKS - 1], r[1:2]) for r in mate]
    mate_own = (mate_outer[0], jnp.exp2(mate_outer[1]), discount(mate_outer[2]), mate_outer[3])
    mate_sums = added(
        pair_sums(mate_own, *far_block(*mate_outer)), pair_sums(mate_own, *far_block(*mate_next))
    )
    outer_copy.wait_recv()
    outer_turned[:, MAXQ:] = outer_in[...].T.astype(BF16)
    outer_features[MAXQ:, :] = outer_in[...].astype(BF16)
    mate_leaves = info_in[4]
    outer_masks = [
        leaf_mask(pick(leaves[:1], leaves[BLOCKS - 1 :])),
        leaf_mask(pick(mate_leaves[BLOCKS - 1 :], mate_leaves[:1])),
    ]
    in_leaf[:, DEEP + MAXQ : ROWS] = outer_masks[0]
    in_leaf[:, ROWS : ROWS + MAXQ] = outer_masks[1]

    for slot in range(2):
        remote(edge.at[0], halo.at[slot], halo_send.at[0], halo_recv.at[slot], plane(0, 0, 1)).wait_recv()
    first_chip = (z == 0) & (y_lo == 0) & (x == 0) & (y_hi == 0)
    last_chip = (z == depth - 1) & (y_lo == 1) & (x == 3) & (y_hi == 1)
    top = iota((8, MAXQ), 0) == 0
    was = jnp.where(top & first_chip, -1.0, halo[0])
    will = jnp.where(top & last_chip, -1.0, halo[1])
    near = pick(was, will)
    far = pick(will, was)
    outer = [pick(r[:1], r[BLOCKS - 1 :]) for r in own]
    outer_sums = tuple(pick(a, b) for a, b in zip(sums[0], sums[BLOCKS - 1]))
    ends = [
        normalized(added(outer_sums, pair_sums(outer, *far_block(*[near[c : c + 1] for c in range(4)])))),
        normalized(added(mate_sums, pair_sums(mate_own, *far_block(*[far[c : c + 1] for c in range(4)])))),
    ]
    out[0, pl.ds(core * (BLOCKS - 1), 1), :] = ends[0][0]
    for k in range(2):
        place = slice(MAXQ * k, MAXQ * (k + 1))
        outer_weighted[:, place] = (outer_turned[:, place].astype(F32) * ends[k][1]).astype(BF16)
    small = leaf_sums(
        outer_masks, [e[0] for e in ends], [e[1] for e in ends], outer_features[...], outer_weighted[...]
    )
    for k in range(6):
        end_sums[k] = small[k]

    def outer_leaf(number):
        mixed, diag, low = leaf_gram(
            in_leaf[pl.ds(number, 1), DEEP + MAXQ : ROWS + MAXQ], outer_features[...], outer_weighted[...]
        )
        extra = stacked([end_sums[k, pl.ds(number, 1), :] for k in range(6)] + [diag])
        first = jnp.concatenate(
            [mixed[:64], extra, mixed[64:], jnp.zeros((8, HALF), F32)], axis=0
        )
        return first, low

    def p1x_copy(t):
        j, d = turn(t), lax.div(t, 2) + 1
        return remote(
            first_sum.at[j],
            first_in.at[d - 1, lax.rem(t, 2)],
            p1x_send.at[j],
            p1x_recv.at[d - 1, lax.rem(t, 2)],
            device(z, y, ahead(x, d, 4), core),
        )

    def row_of(j):
        return 2 * lax.rem(j, 2) + lax.rem(lax.div(j, 2), 2)

    def p1y_copy(j):
        d = lax.rem(row_of(j) - y + 4, 4)
        return remote(
            second_sum.at[j],
            second_in.at[lax.rem(d + 3, 4), lax.div(j, 4)],
            p1y_send.at[j],
            p1y_recv.at[lax.rem(d + 3, 4), lax.div(j, 4)],
            device(z, row_of(j), x, core),
        )

    def for_own(t, carry):
        j = turn(t)
        first, second = outer_leaf(8 * core + j)
        pair_copy(j).wait_recv()
        first_sum[j] = first_sum[j] + first + pair_in[j, :144, :]
        second_sum[j] = second_sum[j] + second + pair_in[j, 144:, :]

        @pl.when(t < 6)
        def _():
            p1x_copy(t).start()

        @pl.when(row_of(j) != y)
        def _():
            p1y_copy(j).start()

        return carry

    lax.fori_loop(0, 8, for_own, 0)

    for h in range(2):
        for d in range(1, 4):
            p1x_copy(2 * (d - 1) + h).wait_recv()
        total = first_sum[2 * x + h] + first_in[0, h] + first_in[1, h] + first_in[2, h]
        first_part[2 * h] = total[:72]
        first_part[2 * h + 1] = total[72:]

    def p2x_copy(d):
        at = ahead(y, d, 4)
        return remote(
            first_part.at[at], first_in2.at[d - 1], p2x_send.at[d - 1], p2x_recv.at[d - 1],
            device(z, at, x, core),
        )

    def p2y_copy(d):
        at = ahead(x, d, 4)
        return remote(
            second_part.at[at], second_in2.at[d - 1], p2y_send.at[d - 1], p2y_recv.at[d - 1],
            device(z, y, at, core),
        )

    for d in (2, 1, 3):
        p2x_copy(d).start()
    for u in range(2):
        for d in range(1, 4):
            remote(
                second_sum.at[0], second_in.at[d - 1, u], p1y_send.at[0], p1y_recv.at[d - 1, u],
                device(z, ahead(y, d, 4), x, core),
            ).wait_recv()
        j = 4 * u + 2 * y_lo + y_hi
        total = second_sum[j] + second_in[0, u] + second_in[1, u] + second_in[2, u]
        second_part[2 * u] = total[:64]
        second_part[2 * u + 1] = total[64:]
    for d in (2, 1, 3):
        p2y_copy(d).start()

    for d in range(1, 4):
        p2x_copy(d).wait_recv()
    total = first_part[y] + first_in2[0] + first_in2[1] + first_in2[2]
    slab[:, 0:8, :] = total[:64].reshape(8, 8, HALF)
    slab[:, 8:16, :] = jnp.broadcast_to(total[64:][None], (8, 8, HALF))
    for d in range(1, 4):
        p2y_copy(d).wait_recv()
    total = second_part[x] + second_in2[0] + second_in2[1] + second_in2[2]
    slab[:, 16:24, :] = total.reshape(8, 8, HALF)

    def z_copy(d):
        at = ahead(z, d, depth)
        return remote(
            slab.at[at], slab_in.at[d - 1], z_send.at[d - 1], z_recv.at[d - 1],
            device(at, y, x, core),
        )

    order = (4, 3, 5, 2, 6, 1, 7)
    for d in order:
        z_copy(d).start()
    for d in order:
        z_copy(d).wait_recv()
    total = slab[z]
    for d in range(1, depth):
        total = total + slab_in[d - 1]
    final[...] = total

    def gx_copy(d):
        at = ahead(z, d, depth)
        return remote(
            final.at[0:16], first_all.at[y_lo, z], gx_send.at[d], gx_recv.at[y_lo, z],
            device(at, 2 * y_hi + x_lo, x, core),
        )

    def gy_copy(d):
        at = ahead(z, d, depth)
        return remote(
            final.at[16:24], second_all.at[x_lo, z], gy_send.at[d], gy_recv.at[x_lo, z],
            device(at, y, 2 * x_hi + y_lo, core),
        )

    for d in order:
        gx_copy(d).start()
        gy_copy(d).start()

    @pl.when(jnp.logical_not(solver))
    def _():
        gx_copy(0).start()
        gy_copy(0).start()

    def w_copy(k):
        to = plane(*in_plane[k])
        return remote(coef, coefs.at[8 * core + 2 * x + y_hi], w_send.at[k],
                      w_recv.at[8 * core + 2 * x + y_hi], to)

    @pl.when(solver)
    def _():
        pltpu.make_async_copy(final.at[0:16], first_all.at[y_lo, z], gx_recv.at[y_lo, z]).start()
        pltpu.make_async_copy(final.at[16:24], second_all.at[x_lo, z], gy_recv.at[x_lo, z]).start()
        for s in range(2):
            for k in range(8):
                remote(final.at[0:16], first_all.at[s, k], gx_send.at[0], gx_recv.at[s, k],
                       plane(0, 0, 1)).wait_recv()
                remote(final.at[16:24], second_all.at[s, k], gy_send.at[0], gy_recv.at[s, k],
                       plane(0, 0, 1)).wait_recv()
        mixed = first_all[:, :, 0:8, :].reshape(HALF, HALF)
        extra = first_all[0, 0, 8:16, :]
        low = second_all[...].reshape(HALF, HALF)
        coef[...] = solved(mixed, extra, low)
        for k in range(len(in_plane)):
            w_copy(k).start()
        mine = 8 * core + 2 * x + y_hi
        pltpu.make_async_copy(coef, coefs.at[mine], w_recv.at[mine]).start()

    for k in range(LEAVES):
        remote(coef, coefs.at[k], w_send.at[0], w_recv.at[k], plane(0, 0, 1)).wait_recv()
    block = coefs[...]
    weights = jnp.concatenate([block[:, 0, :], block[:, 1, :]], axis=1)
    leaf_output(features, leaf, score, weights, block[:, 2, :], out.at[1], out.at[2])

    def sent(t, carry):
        j = turn(t)
        pair_copy(j).wait_send()

        @pl.when(t < 6)
        def _():
            p1x_copy(t).wait_send()

        @pl.when(row_of(j) != y)
        def _():
            p1y_copy(j).wait_send()

        return carry

    lax.fori_loop(0, 8, sent, 0)
    for copy in halos + [info_copy, outer_copy]:
        copy.wait_send()
    for d in range(1, 4):
        p2x_copy(d).wait_send()
        p2y_copy(d).wait_send()
    for d in range(1, depth):
        z_copy(d).wait_send()
        gx_copy(d).wait_send()
        gy_copy(d).wait_send()

    @pl.when(jnp.logical_not(solver))
    def _():
        gx_copy(0).wait_send()
        gy_copy(0).wait_send()

    @pl.when(solver)
    def _():
        for k in range(len(in_plane)):
            w_copy(k).wait_send()


def body(features, scores, labels, query_ids, ranks, leaf_ids):
    lines = [x.reshape(BLOCKS, MAXQ) for x in (scores, labels, query_ids, ranks, leaf_ids)]
    dma = pltpu.SemaphoreType.DMA
    tile = lambda *shape: pltpu.VMEM((*shape, HALF), F32)
    out = pl.pallas_call(
        level_kernel,
        out_shape=jax.ShapeDtypeStruct((3, BLOCKS, MAXQ), F32),
        in_specs=[VMEM] * 6,
        out_specs=VMEM,
        scratch_shapes=[
            pltpu.VMEM((F, DEEP), BF16),
            pltpu.VMEM((F, EDGE), BF16),
            pltpu.VMEM((F, EDGE), BF16),
            pltpu.VMEM((EDGE, F), BF16),
            pltpu.VMEM((LEAVES, 2 * ROWS), F32),
            tile(6, LEAVES), tile(6, LEAVES),
            tile(LEAVES, HALF), tile(LEAVES, 8), tile(LEAVES, HALF),
            tile(2, 8), tile(2, 8), tile(5, 8), tile(5, 8),
            pltpu.VMEM((MAXQ, F), F32), pltpu.VMEM((MAXQ, F), F32),
            tile(8, LEAF_ROWS), tile(8, LEAF_ROWS),
            tile(8, 144), tile(8, 128), tile(3, 2, 144), tile(3, 2, 128),
            tile(4, 72), tile(4, 64), tile(3, 72), tile(3, 64),
            tile(8, 24), tile(7, 24), tile(24), tile(2, 8, 16), tile(2, 8, 8), tile(8),
            tile(LEAVES, 8),
            dma((2,)), dma((2,)), dma((2,)), dma((2,)), dma((8,)), dma((8,)),
            dma((8,)), dma((3, 2)), dma((8,)), dma((3, 2)),
            dma((3,)), dma((3,)), dma((3,)), dma((3,)),
            dma((7,)), dma((7,)), dma((8,)), dma((2, 8)), dma((8,)), dma((2, 8)),
            dma((31,)), dma((LEAVES,)),
        ],
        compiler_params=pltpu.CompilerParams(collective_id=0, has_side_effects=True),
    )(features, *lines)
    return out[0].reshape(ROWS), out[1].reshape(ROWS), out[2].reshape(ROWS)


def solution(mesh):
    torus = Mesh(mesh.devices.reshape(mesh.shape["doc"] // 2, 2, 4, 2, 2), AXES)
    spec = P(AXES)
    return jax.shard_map(
        body,
        mesh=torus,
        in_specs=(P(AXES, None), spec, spec, spec, spec, spec),
        out_specs=(spec, spec, spec),
        check_vma=False,
    )
```

```python
import jax
import jax.numpy as jnp
from jax import lax
from jax.experimental import pallas as pl
from jax.experimental.pallas import tpu as pltpu
from jax.sharding import Mesh
from jax.sharding import PartitionSpec as P

LEAVES = 16
MAXQ = 128
ROWS = 1024
BLOCKS = ROWS // MAXQ
F = 256
HALF = 128
LEAF_ROWS = 272
AXES = ("z", "y_lo", "x", "y_hi", "core")
MESH = pl.DeviceIdType.MESH
PIVOTS = 8
INNER = slice(MAXQ, ROWS - MAXQ)
DEEP = ROWS - 2 * MAXQ
EDGE = 2 * MAXQ
LAMBDA = 1.0
SHRINKAGE = 0.1
F32 = jnp.float32
BF16 = jnp.bfloat16
NT = (((1,), (1,)), ((), ()))
VMEM = pl.BlockSpec(memory_space=pltpu.VMEM)


def iota(shape, dim):
    return lax.broadcasted_iota(jnp.int32, shape, dim)


def discount(rank_values):
    return 1.0 / jnp.log2(1.0 + jnp.maximum(rank_values, 1.0))


def stacked(rows):
    width = rows[0].shape[1]
    sub = iota((8, width), 0)
    out = jnp.zeros((8, width), F32)
    for k, row in enumerate(rows):
        out = jnp.where(sub == k, jnp.broadcast_to(row, (8, width)), out)
    return out


def pair_sums(own, far_cols, far_ge):
    query, gain, disc, score = own
    far_query, far_gain, far_disc, far_score = far_cols
    same = far_query == query
    gain_gap = gain - far_gain
    score_gap = score - far_score
    signed = jnp.where(same, gain_gap * jnp.abs(disc - far_disc), 0.0)
    prob = 1.0 / (1.0 + jnp.exp(jnp.where(gain_gap >= 0.0, score_gap, -score_gap)))
    pull = signed * prob
    grad = jnp.sum(pull, axis=0, keepdims=True)
    hess = jnp.sum(jnp.abs(pull) * (1.0 - prob), axis=0, keepdims=True)
    mates = jnp.where(same, 1.0, 0.0).astype(BF16)
    counts = jnp.dot(far_ge, mates, preferred_element_type=F32)
    return grad, hess, counts


def far_block(query, label, rank, score):
    gain = jnp.exp2(label)
    disc = discount(rank)
    turned = stacked([query, gain, disc, score]).T
    cols = [jnp.broadcast_to(turned[:, c : c + 1], (MAXQ, MAXQ)) for c in range(4)]
    level = (iota((16, MAXQ), 0) + 1).astype(F32)
    at_least = jnp.where(jnp.broadcast_to(label, (16, MAXQ)) >= level, 1.0, 0.0).astype(BF16)
    return cols, at_least


def own_rows(query_ref, label_ref, rank_ref, score_ref):
    query = query_ref[...].astype(F32)
    label = label_ref[...].astype(F32)
    rank = rank_ref[...].astype(F32)
    return query, label, rank, score_ref[...]


def meet(own, sums, k, far):
    new = pair_sums([x[k : k + 1, :] for x in own], *far)
    sums[k] = new if sums[k] is None else tuple(a + b for a, b in zip(sums[k], new))


def lambdas_within(rows):
    query, label, rank, score = rows
    own = (query, jnp.exp2(label), discount(rank), score)
    sums = [None] * BLOCKS
    for j in range(BLOCKS):
        far = far_block(*[x[j : j + 1, :] for x in rows])
        for k in (j - 1, j, j + 1):
            if 0 <= k < BLOCKS:
                meet(own, sums, k, far)
    return own, sums


def added(first, second):
    return tuple(a + b for a, b in zip(first, second))


def normalized(sums):
    pull, push, counts = sums
    position = (iota((MAXQ, MAXQ), 0) + 1).astype(F32)
    disc_at = discount(position)
    ideal = jnp.zeros((1, MAXQ), F32)
    for level in range(4):
        inside = jnp.where(position <= counts[level : level + 1, :], disc_at, 0.0)
        ideal = ideal + float(2**level) * jnp.sum(inside, axis=0, keepdims=True)
    inverse = 1.0 / jnp.maximum(ideal, 1.0)
    return -inverse * pull, inverse * push


def leaf_mask(leaf):
    wide = (LEAVES, MAXQ)
    return jnp.where(jnp.broadcast_to(leaf, wide) == iota(wide, 0).astype(F32), 1.0, 0.0)


def leaf_sums(in_leaf, grads, hess, features, weighted):
    total = lambda parts: jnp.broadcast_to(
        jnp.sum(tree_sum(parts), axis=1, keepdims=True), (LEAVES, MAXQ)
    )
    low = jnp.concatenate([(m * g).astype(BF16) for m, g in zip(in_leaf, grads)], axis=1)
    moment = jnp.dot(low, features, preferred_element_type=F32)
    masks = jnp.concatenate([m.astype(BF16) for m in in_leaf], axis=1)
    hsum = lax.dot_general(masks, weighted, NT, preferred_element_type=F32)
    return [
        hsum[:, :HALF],
        hsum[:, HALF:],
        moment[:, :HALF],
        moment[:, HALF:],
        total([m * h for m, h in zip(in_leaf, hess)]),
        total([m * g for m, g in zip(in_leaf, grads)]),
    ]


def leaf_gram(mask, features, weighted):
    n = features.shape[0]
    own = (weighted.reshape(16, 16, n) * jnp.broadcast_to(mask, (16, n)).astype(BF16)[None])
    gram = jnp.dot(own.reshape(F, n), features, preferred_element_type=F32)
    row = iota((HALF, HALF), 0)
    col = iota((HALF, HALF), 1)
    last = gram[HALF:, HALF:]
    mixed = jnp.where(col <= row, gram[:HALF, :HALF], last)
    diag = jnp.sum(jnp.where(col == row, last, 0.0), axis=0, keepdims=True)
    return mixed, diag, gram[HALF:, :HALF]


def dotted(a, b, dims=(((1,), (0,)), ((), ()))):
    return lax.dot_general(
        a, b, dims, precision=lax.Precision.HIGHEST, preferred_element_type=F32
    )


def tree_sum(terms):
    while len(terms) > 1:
        terms = [sum(terms[k : k + 2][1:], terms[k]) for k in range(0, len(terms), 2)]
    return terms[0]


def small_inverse(d):
    p = len(d)
    if p == 1:
        return [[1.0 / d[0][0]]]
    if p == 2:
        a, b, c = d[0][0], d[0][1], d[1][1]
        r = 1.0 / (a * c - b * b)
        n = -b * r
        return [[c * r, n], [n, a * r]]
    h = p // 2

    def dot(xs, ys):
        return tree_sum([x * y for x, y in zip(xs, ys)])

    first = small_inverse([line[:h] for line in d[:h]])
    side = [line[h:] for line in d[:h]]
    u = [[dot(first[i], [side[m][j] for m in range(h)]) for j in range(h)] for i in range(h)]
    rest = [[None] * h for _ in range(h)]
    for i in range(h):
        for j in range(i, h):
            rest[i][j] = rest[j][i] = d[h + i][h + j] - dot(
                [side[m][i] for m in range(h)], [u[m][j] for m in range(h)]
            )
    last = small_inverse(rest)
    out = [[None] * p for _ in range(p)]
    for i in range(h):
        for j in range(h):
            out[h + i][h + j] = last[i][j]
            out[i][h + j] = out[h + j][i] = -dot(u[i], [last[m][j] for m in range(h)])
    for i in range(h):
        for j in range(i, h):
            out[i][j] = out[j][i] = first[i][j] - dot(
                [out[i][h + m] for m in range(h)], [u[j][m] for m in range(h)]
            )
    return out


def spd_inverse(m, p):
    n = m.shape[0]
    lane = iota((8, n), 1)
    sub = iota((8, n), 0)
    kept = jnp.where(iota((n, n), 0) == iota((n, n), 1), m, 0.0)
    unit = lax.rsqrt(jnp.sum(kept, axis=0, keepdims=True))
    unit = unit * lax.rsqrt(jnp.sum(kept, axis=1, keepdims=True))
    m = m * unit
    for k in range(0, n, p):
        top = k // 8 * 8
        cols = [jnp.broadcast_to(m[:, k + b : k + b + 1], m.shape) for b in range(p)]
        rows = [jnp.broadcast_to(m[k + a : k + a + 1, :], (8, n)) for a in range(p)]
        d = [[None] * p for _ in range(p)]
        for a in range(p):
            for b in range(a, p):
                d[a][b] = d[b][a] = jnp.broadcast_to(cols[b][k + a : k + a + 1, :], (8, n))
        v = small_inverse(d)
        scaled = []
        for a in range(p):
            r = tree_sum([v[a][b] * rows[b] for b in range(p)])
            for b in range(p):
                r = jnp.where(lane == k + b, v[a][b], r)
            scaled.append(r)
        pivot = (lane >= k) & (lane < k + p)
        tiles = {}
        for t in [(k + p) // 8 * 8 % n] + [t for t in range(0, n, 8) if t != (k + p) // 8 * 8 % n]:
            tile = jnp.where(pivot, 0.0, m[t : t + 8, :])
            tile = tile - tree_sum([cols[a][t : t + 8, :] * scaled[a] for a in range(p)])
            if t == top:
                for a in range(p):
                    tile = jnp.where(sub == k - top + a, scaled[a], tile)
            tiles[t] = tile
        m = jnp.concatenate([tiles[t] for t in range(0, n, 8)], axis=0)
    return m * unit


def solved(mixed, extra, low):
    row = iota((HALF, HALF), 0)
    col = iota((HALF, HALF), 1)
    turned = mixed.T
    hsum = [extra[0:1, :], extra[1:2, :]]
    moment = [extra[2:3, :], extra[3:4, :]]
    htotal, gtotal, diag = extra[4:5, :], extra[5:6, :], extra[6:7, :]
    share = 1.0 / (htotal + LAMBDA)
    scaled = [h * share for h in hsum]
    across = stacked(hsum).T
    over = [jnp.broadcast_to(across[:, k : k + 1], (HALF, HALF)) for k in range(2)]
    unit = jnp.where(row == col, LAMBDA, 0.0)
    a11 = jnp.where(col <= row, mixed, turned) + unit - over[0] * scaled[0]
    a21 = low - over[1] * scaled[0]
    a22 = jnp.where(col > row, mixed, jnp.where(col < row, turned, diag))
    a22 = a22 + unit - over[1] * scaled[1]
    side = [scaled[k] * gtotal - moment[k] for k in range(2)]
    inv1 = spd_inverse(a11, PIVOTS)
    z = dotted(a21, inv1)
    inv2 = spd_inverse(a22 - dotted(z, a21, NT), PIVOTS)
    b1 = jnp.broadcast_to(side[0], (8, HALF))
    b2 = jnp.broadcast_to(side[1], (8, HALF))
    w2 = dotted(b2 - dotted(b1, z, NT), inv2)
    w1 = dotted(b1, inv1) - dotted(w2, z)
    total = jnp.sum(hsum[0] * w1 + hsum[1] * w2, axis=1, keepdims=True)
    c = -(gtotal + total) * share
    return stacked([w1[0:1], w2[0:1], c[0:1]])


def leaf_output(features_ref, leaf_ref, score_ref, weights, intercepts, tree_ref, new_ref):
    high = weights.astype(BF16)
    left = weights - high.astype(F32)
    mid = left.astype(BF16)
    low = (left - mid.astype(F32)).astype(BF16)
    parts = jnp.concatenate([high, mid, low], axis=0)
    sums = lax.dot_general(parts, features_ref[...], NT, preferred_element_type=F32)
    per_leaf = sums[:16] + sums[16:32] + sums[32:48]
    leaf = leaf_ref[...]
    for k in range(BLOCKS):
        rows = slice(MAXQ * k, MAXQ * (k + 1))
        own = jnp.broadcast_to(leaf[k : k + 1, :], (LEAVES, MAXQ)) == iota((LEAVES, MAXQ), 0)
        tree = jnp.sum(
            jnp.where(own, per_leaf[:, rows] + intercepts, 0.0), axis=0, keepdims=True
        )
        tree_ref[k : k + 1, :] = tree
        new_ref[k : k + 1, :] = score_ref[k : k + 1, :] + SHRINKAGE * tree


def position():
    z, y_lo, x, y_hi, core = [lax.axis_index(a) for a in AXES]
    return z, 2 * y_hi + y_lo, x, core


def device(z, y, x, core):
    return (z, lax.rem(y, 2), x, lax.div(y, 2), core)


def neighbour(by):
    index = jnp.int32(0)
    total = 1
    for a in AXES:
        index = index * lax.axis_size(a) + lax.axis_index(a)
        total *= lax.axis_size(a)
    index = lax.rem(index + by + total, total)
    place = []
    for a in reversed(AXES):
        place.append(lax.rem(index, lax.axis_size(a)))
        index = lax.div(index, lax.axis_size(a))
    return tuple(reversed(place))


def ahead(value, by, size):
    return lax.rem(value + by, size)


def level_kernel(
    features, score, label, query, rank, leaf,
    out,
    inner_weighted, outer_turned, outer_weighted, outer_features, in_leaf, sums_ref, end_sums,
    inner_mixed, inner_diag, inner_low,
    edge, halo, info, info_in, outer_out, outer_in,
    pair_out, pair_in,
    first_sum, second_sum, first_in, second_in,
    first_part, second_part, first_in2, second_in2,
    slab, slab_in, final, first_all, second_all, coef, coefs,
    halo_send, halo_recv, mate_send, mate_recv, pair_send, pair_recv,
    p1x_send, p1x_recv, p1y_send, p1y_recv,
    p2x_send, p2x_recv, p2y_send, p2y_recv,
    z_send, z_recv, gx_send, gx_recv, gy_send, gy_recv,
    w_send, w_recv,
):
    z, y, x, core = position()
    depth = lax.axis_size("z")
    y_lo, x_lo = lax.rem(y, 2), lax.rem(x, 2)
    y_hi, x_hi = lax.div(y, 2), lax.div(x, 2)
    y_pair, x_pair = y + 1 - 2 * y_lo, x + 1 - 2 * x_lo
    other = 1 - core
    solver = x_lo == y_lo
    in_plane = [
        (dx, dy, dc) for dx in (2, 1, 3, 0) for dy in (2, 1, 3, 0) for dc in (1, 0) if dx or dy or dc
    ]

    def plane(dx, dy, dc):
        return device(z, ahead(y, dy, 4), ahead(x, dx, 4), ahead(core, dc, 2))

    def pick(a, b):
        return jnp.where(core == 0, a, b)

    barrier = pltpu.get_barrier_semaphore()
    partners = [neighbour(by - core) for by in (-2, -1, 2, 3)] + [plane(*d) for d in in_plane]
    for d in range(1, depth):
        at = ahead(z, d, depth)
        partners += [device(at, y, x, core), device(at, y_pair, x, core), device(at, y, x_pair, core)]
    for partner in partners:
        pl.semaphore_signal(barrier, inc=1, device_id=partner, device_id_type=MESH)

    def remote(src, dst, send, recv, to):
        return pltpu.make_async_remote_copy(
            src_ref=src, dst_ref=dst, send_sem=send, recv_sem=recv, device_id=to, device_id_type=MESH
        )

    rows = own_rows(query, label, rank, score)
    leaves = leaf[...].astype(F32)
    edge[0] = stacked([r[BLOCKS - 1 : BLOCKS, :] for r in rows])
    edge[1] = stacked([r[0:1, :] for r in rows])
    for k in range(4):
        info[k] = rows[k]
    info[4] = leaves
    outer_start = pl.multiple_of(core * (ROWS - MAXQ), MAXQ)
    middle_start = pl.multiple_of(other * (ROWS - MAXQ), MAXQ)
    outer_out[...] = features[pl.ds(outer_start, MAXQ), :].astype(F32)
    own, sums = lambdas_within(rows)

    inner = range(1, BLOCKS - 1)
    grads, hess = [], []
    for b in inner:
        turned = features[MAXQ * b : MAXQ * (b + 1), :].astype(F32).T
        g, h = normalized(sums[b])
        grads.append(g)
        hess.append(h)
        out[0, b : b + 1, :] = g
        inner_weighted[:, MAXQ * (b - 1) : MAXQ * b] = (turned * h).astype(BF16)
    masks = [leaf_mask(leaves[b : b + 1, :]) for b in inner]
    for b in inner:
        in_leaf[:, MAXQ * (b - 1) : MAXQ * b] = masks[b - 1]
    small = leaf_sums(masks, grads, hess, features[INNER, :], inner_weighted[...])
    for k in range(6):
        sums_ref[k] = small[k]
    middle_turned = outer_weighted.at[:, :MAXQ]
    middle_turned[...] = features[pl.ds(middle_start, MAXQ), :].astype(F32).T.astype(BF16)
    outer_turned[:, :MAXQ] = outer_out[...].T.astype(BF16)
    outer_features[:MAXQ, :] = features[pl.ds(outer_start, MAXQ), :]

    def inner_leaf(number, carry):
        mixed, diag, low = leaf_gram(
            in_leaf[pl.ds(number, 1), :DEEP], features[INNER, :], inner_weighted[...]
        )
        inner_mixed[number] = mixed
        inner_diag[number] = jnp.broadcast_to(diag, (8, HALF))
        inner_low[number] = low
        return carry

    lax.fori_loop(0, LEAVES, inner_leaf, 0)
    pl.semaphore_wait(barrier, len(partners))

    halos = [
        remote(
            edge.at[other], halo.at[other], halo_send.at[k], halo_recv.at[other],
            neighbour(pick(-2, 1) + k),
        )
        for k in range(2)
    ]
    for copy in halos:
        copy.start()
    info_copy = remote(info, info_in, mate_send.at[0], mate_recv.at[0], plane(0, 0, 1))
    outer_copy = remote(outer_out, outer_in, mate_send.at[1], mate_recv.at[1], plane(0, 0, 1))
    info_copy.start()
    outer_copy.start()
    info_copy.wait_recv()

    mate = [info_in[k] for k in range(4)]
    beside = far_block(*[pick(r[:1], r[BLOCKS - 1 :]) for r in mate])
    middle = [pick(r[BLOCKS - 1 :], r[:1]) for r in own]
    middle_sums = tuple(pick(a, b) for a, b in zip(sums[BLOCKS - 1], sums[0]))
    g, h = normalized(added(middle_sums, pair_sums(middle, *beside)))
    out[0, pl.ds(other * (BLOCKS - 1), 1), :] = g
    middle_weighted = (middle_turned[...].astype(F32) * h).astype(BF16)
    middle_mask = leaf_mask(pick(leaves[BLOCKS - 1 :], leaves[:1]))
    middle_features = features[pl.ds(middle_start, MAXQ), :]
    in_leaf[:, DEEP : DEEP + MAXQ] = middle_mask
    small = leaf_sums([middle_mask], [g], [h], middle_features, middle_weighted)
    for k in range(6):
        sums_ref[k] = sums_ref[k] + small[k]
    outer_weighted[:, :MAXQ] = middle_weighted

    def chip_leaf(number):
        mixed, diag, low = leaf_gram(
            in_leaf[pl.ds(number, 1), DEEP : DEEP + 2 * MAXQ][:, :MAXQ],
            features[pl.ds(middle_start, MAXQ), :],
            outer_weighted[:, :MAXQ],
        )
        mixed = mixed + inner_mixed[number]
        extra = [sums_ref[k, pl.ds(number, 1), :] for k in range(6)]
        extra = stacked(extra + [diag + inner_diag[number, 0:1, :]])
        first = jnp.concatenate(
            [mixed[:64], extra, mixed[64:], jnp.zeros((8, HALF), F32)], axis=0
        )
        return first, low + inner_low[number]

    def turn(t):
        return lax.rem(2 * (x + 1) + t, 8)

    def pair_copy(j):
        return remote(
            pair_out.at[j], pair_in.at[j], pair_send.at[j], pair_recv.at[j], plane(0, 0, 1)
        )

    def for_other(t, carry):
        j = turn(t)
        first, second = chip_leaf(8 * other + j)
        pair_out[j, :144, :] = first
        pair_out[j, 144:, :] = second
        pair_copy(j).start()
        return carry

    lax.fori_loop(0, 8, for_other, 0)

    def for_own_rows(t, carry):
        j = turn(t)
        first, second = chip_leaf(8 * core + j)
        first_sum[j] = first
        second_sum[j] = second
        return carry

    lax.fori_loop(0, 8, for_own_rows, 0)
    mate_outer = [pick(r[BLOCKS - 1 :], r[:1]) for r in mate]
    mate_next = [pick(r[BLOCKS - 2 : BLOCKS - 1], r[1:2]) for r in mate]
    mate_own = (mate_outer[0], jnp.exp2(mate_outer[1]), discount(mate_outer[2]), mate_outer[3])
    mate_sums = added(
        pair_sums(mate_own, *far_block(*mate_outer)), pair_sums(mate_own, *far_block(*mate_next))
    )
    outer_copy.wait_recv()
    outer_turned[:, MAXQ:] = outer_in[...].T.astype(BF16)
    outer_features[MAXQ:, :] = outer_in[...].astype(BF16)
    mate_leaves = info_in[4]
    outer_masks = [
        leaf_mask(pick(leaves[:1], leaves[BLOCKS - 1 :])),
        leaf_mask(pick(mate_leaves[BLOCKS - 1 :], mate_leaves[:1])),
    ]
    in_leaf[:, DEEP + MAXQ : ROWS] = outer_masks[0]
    in_leaf[:, ROWS : ROWS + MAXQ] = outer_masks[1]

    for slot in range(2):
        remote(edge.at[0], halo.at[slot], halo_send.at[0], halo_recv.at[slot], plane(0, 0, 1)).wait_recv()
    first_chip = (z == 0) & (y_lo == 0) & (x == 0) & (y_hi == 0)
    last_chip = (z == depth - 1) & (y_lo == 1) & (x == 3) & (y_hi == 1)
    top = iota((8, MAXQ), 0) == 0
    was = jnp.where(top & first_chip, -1.0, halo[0])
    will = jnp.where(top & last_chip, -1.0, halo[1])
    near = pick(was, will)
    far = pick(will, was)
    outer = [pick(r[:1], r[BLOCKS - 1 :]) for r in own]
    outer_sums = tuple(pick(a, b) for a, b in zip(sums[0], sums[BLOCKS - 1]))
    ends = [
        normalized(added(outer_sums, pair_sums(outer, *far_block(*[near[c : c + 1] for c in range(4)])))),
        normalized(added(mate_sums, pair_sums(mate_own, *far_block(*[far[c : c + 1] for c in range(4)])))),
    ]
    out[0, pl.ds(core * (BLOCKS - 1), 1), :] = ends[0][0]
    for k in range(2):
        place = slice(MAXQ * k, MAXQ * (k + 1))
        outer_weighted[:, place] = (outer_turned[:, place].astype(F32) * ends[k][1]).astype(BF16)
    small = leaf_sums(
        outer_masks, [e[0] for e in ends], [e[1] for e in ends], outer_features[...], outer_weighted[...]
    )
    for k in range(6):
        end_sums[k] = small[k]

    def outer_leaf(number):
        mixed, diag, low = leaf_gram(
            in_leaf[pl.ds(number, 1), DEEP + MAXQ : ROWS + MAXQ], outer_features[...], outer_weighted[...]
        )
        extra = stacked([end_sums[k, pl.ds(number, 1), :] for k in range(6)] + [diag])
        first = jnp.concatenate(
            [mixed[:64], extra, mixed[64:], jnp.zeros((8, HALF), F32)], axis=0
        )
        return first, low

    def p1x_copy(t):
        j, d = turn(t), lax.div(t, 2) + 1
        return remote(
            first_sum.at[j],
            first_in.at[d - 1, lax.rem(t, 2)],
            p1x_send.at[j],
            p1x_recv.at[d - 1, lax.rem(t, 2)],
            device(z, y, ahead(x, d, 4), core),
        )

    def row_of(j):
        return 2 * lax.rem(j, 2) + lax.rem(lax.div(j, 2), 2)

    def p1y_copy(j):
        d = lax.rem(row_of(j) - y + 4, 4)
        return remote(
            second_sum.at[j],
            second_in.at[lax.rem(d + 3, 4), lax.div(j, 4)],
            p1y_send.at[j],
            p1y_recv.at[lax.rem(d + 3, 4), lax.div(j, 4)],
            device(z, row_of(j), x, core),
        )

    def for_own(t, carry):
        j = turn(t)
        first, second = outer_leaf(8 * core + j)
        pair_copy(j).wait_recv()
        first_sum[j] = first_sum[j] + first + pair_in[j, :144, :]
        second_sum[j] = second_sum[j] + second + pair_in[j, 144:, :]

        @pl.when(t < 6)
        def _():
            p1x_copy(t).start()

        @pl.when(row_of(j) != y)
        def _():
            p1y_copy(j).start()

        return carry

    lax.fori_loop(0, 8, for_own, 0)

    for h in range(2):
        for d in range(1, 4):
            p1x_copy(2 * (d - 1) + h).wait_recv()
        total = first_sum[2 * x + h] + first_in[0, h] + first_in[1, h] + first_in[2, h]
        first_part[2 * h] = total[:72]
        first_part[2 * h + 1] = total[72:]

    def p2x_copy(d):
        at = ahead(y, d, 4)
        return remote(
            first_part.at[at], first_in2.at[d - 1], p2x_send.at[d - 1], p2x_recv.at[d - 1],
            device(z, at, x, core),
        )

    def p2y_copy(d):
        at = ahead(x, d, 4)
        return remote(
            second_part.at[at], second_in2.at[d - 1], p2y_send.at[d - 1], p2y_recv.at[d - 1],
            device(z, y, at, core),
        )

    for d in (2, 1, 3):
        p2x_copy(d).start()
    for u in range(2):
        for d in range(1, 4):
            remote(
                second_sum.at[0], second_in.at[d - 1, u], p1y_send.at[0], p1y_recv.at[d - 1, u],
                device(z, ahead(y, d, 4), x, core),
            ).wait_recv()
        j = 4 * u + 2 * y_lo + y_hi
        total = second_sum[j] + second_in[0, u] + second_in[1, u] + second_in[2, u]
        second_part[2 * u] = total[:64]
        second_part[2 * u + 1] = total[64:]
    for d in (2, 1, 3):
        p2y_copy(d).start()

    for d in range(1, 4):
        p2x_copy(d).wait_recv()
    total = first_part[y] + first_in2[0] + first_in2[1] + first_in2[2]
    slab[:, 0:8, :] = total[:64].reshape(8, 8, HALF)
    slab[:, 8:16, :] = jnp.broadcast_to(total[64:][None], (8, 8, HALF))
    for d in range(1, 4):
        p2y_copy(d).wait_recv()
    total = second_part[x] + second_in2[0] + second_in2[1] + second_in2[2]
    slab[:, 16:24, :] = total.reshape(8, 8, HALF)

    def z_copy(d):
        at = ahead(z, d, depth)
        return remote(
            slab.at[at], slab_in.at[d - 1], z_send.at[d - 1], z_recv.at[d - 1],
            device(at, y, x, core),
        )

    order = (4, 3, 5, 2, 6, 1, 7)
    for d in order:
        z_copy(d).start()
    for d in order:
        z_copy(d).wait_recv()
    total = slab[z]
    for d in range(1, depth):
        total = total + slab_in[d - 1]
    final[...] = total

    def gx_copy(d):
        at = ahead(z, d, depth)
        return remote(
            final.at[0:16], first_all.at[y_lo, z], gx_send.at[d], gx_recv.at[y_lo, z],
            device(at, 2 * y_hi + x_lo, x, core),
        )

    def gy_copy(d):
        at = ahead(z, d, depth)
        return remote(
            final.at[16:24], second_all.at[x_lo, z], gy_send.at[d], gy_recv.at[x_lo, z],
            device(at, y, 2 * x_hi + y_lo, core),
        )

    for d in order:
        gx_copy(d).start()
        gy_copy(d).start()

    @pl.when(jnp.logical_not(solver))
    def _():
        gx_copy(0).start()
        gy_copy(0).start()

    def w_copy(k):
        to = plane(*in_plane[k])
        return remote(coef, coefs.at[8 * core + 2 * x + y_hi], w_send.at[k],
                      w_recv.at[8 * core + 2 * x + y_hi], to)

    @pl.when(solver)
    def _():
        pltpu.make_async_copy(final.at[0:16], first_all.at[y_lo, z], gx_recv.at[y_lo, z]).start()
        pltpu.make_async_copy(final.at[16:24], second_all.at[x_lo, z], gy_recv.at[x_lo, z]).start()
        for s in range(2):
            for k in range(8):
                remote(final.at[0:16], first_all.at[s, k], gx_send.at[0], gx_recv.at[s, k],
                       plane(0, 0, 1)).wait_recv()
                remote(final.at[16:24], second_all.at[s, k], gy_send.at[0], gy_recv.at[s, k],
                       plane(0, 0, 1)).wait_recv()
        mixed = first_all[:, :, 0:8, :].reshape(HALF, HALF)
        extra = first_all[0, 0, 8:16, :]
        low = second_all[...].reshape(HALF, HALF)
        coef[...] = solved(mixed, extra, low)
        for k in range(len(in_plane)):
            w_copy(k).start()
        mine = 8 * core + 2 * x + y_hi
        pltpu.make_async_copy(coef, coefs.at[mine], w_recv.at[mine]).start()

    for k in range(LEAVES):
        remote(coef, coefs.at[k], w_send.at[0], w_recv.at[k], plane(0, 0, 1)).wait_recv()
    block = coefs[...]
    weights = jnp.concatenate([block[:, 0, :], block[:, 1, :]], axis=1)
    leaf_output(features, leaf, score, weights, block[:, 2, :], out.at[1], out.at[2])

    def sent(t, carry):
        j = turn(t)
        pair_copy(j).wait_send()

        @pl.when(t < 6)
        def _():
            p1x_copy(t).wait_send()

        @pl.when(row_of(j) != y)
        def _():
            p1y_copy(j).wait_send()

        return carry

    lax.fori_loop(0, 8, sent, 0)
    for copy in halos + [info_copy, outer_copy]:
        copy.wait_send()
    for d in range(1, 4):
        p2x_copy(d).wait_send()
        p2y_copy(d).wait_send()
    for d in range(1, depth):
        z_copy(d).wait_send()
        gx_copy(d).wait_send()
        gy_copy(d).wait_send()

    @pl.when(jnp.logical_not(solver))
    def _():
        gx_copy(0).wait_send()
        gy_copy(0).wait_send()

    @pl.when(solver)
    def _():
        for k in range(len(in_plane)):
            w_copy(k).wait_send()


def body(features, scores, labels, query_ids, ranks, leaf_ids):
    lines = [x.reshape(BLOCKS, MAXQ) for x in (scores, labels, query_ids, ranks, leaf_ids)]
    dma = pltpu.SemaphoreType.DMA
    tile = lambda *shape: pltpu.VMEM((*shape, HALF), F32)
    out = pl.pallas_call(
        level_kernel,
        out_shape=jax.ShapeDtypeStruct((3, BLOCKS, MAXQ), F32),
        in_specs=[VMEM] * 6,
        out_specs=VMEM,
        scratch_shapes=[
            pltpu.VMEM((F, DEEP), BF16),
            pltpu.VMEM((F, EDGE), BF16),
            pltpu.VMEM((F, EDGE), BF16),
            pltpu.VMEM((EDGE, F), BF16),
            pltpu.VMEM((LEAVES, 2 * ROWS), F32),
            tile(6, LEAVES), tile(6, LEAVES),
            tile(LEAVES, HALF), tile(LEAVES, 8), tile(LEAVES, HALF),
            tile(2, 8), tile(2, 8), tile(5, 8), tile(5, 8),
            pltpu.VMEM((MAXQ, F), F32), pltpu.VMEM((MAXQ, F), F32),
            tile(8, LEAF_ROWS), tile(8, LEAF_ROWS),
            tile(8, 144), tile(8, 128), tile(3, 2, 144), tile(3, 2, 128),
            tile(4, 72), tile(4, 64), tile(3, 72), tile(3, 64),
            tile(8, 24), tile(7, 24), tile(24), tile(2, 8, 16), tile(2, 8, 8), tile(8),
            tile(LEAVES, 8),
            dma((2,)), dma((2,)), dma((2,)), dma((2,)), dma((8,)), dma((8,)),
            dma((8,)), dma((3, 2)), dma((8,)), dma((3, 2)),
            dma((3,)), dma((3,)), dma((3,)), dma((3,)),
            dma((7,)), dma((7,)), dma((8,)), dma((2, 8)), dma((8,)), dma((2, 8)),
            dma((31,)), dma((LEAVES,)),
        ],
        compiler_params=pltpu.CompilerParams(collective_id=0, has_side_effects=True),
    )(features, *lines)
    return out[0].reshape(ROWS), out[1].reshape(ROWS), out[2].reshape(ROWS)


def solution(mesh):
    torus = Mesh(mesh.devices.reshape(mesh.shape["doc"] // 2, 2, 4, 2, 2), AXES)
    spec = P(AXES)
    return jax.shard_map(
        body,
        mesh=torus,
        in_specs=(P(AXES, None), spec, spec, spec, spec, spec),
        out_specs=(spec, spec, spec),
        check_vma=False,
    )
```
